128 devices in a mesh: pipe: 8 (over x, core), expert: 16 (over y, z).
Axes of the slice: x: 4, y: 4, z: 4, core: 2. Of those that a mesh axis runs over, the one named last changes fastest.
Arguments:
- tokens: bfloat16 [4, 64, 3072], P(None, 'expert'), may hold values from -6 to 6
- tangent: bfloat16 [4, 64, 3072], P(None, 'expert'), may hold values from -6 to 6
- w_up: bfloat16 [8, 3072, 32768], P('pipe', None, 'expert'), may hold values from -0.109375 to 0.109375
- w_down: bfloat16 [8, 32768, 3072], P('pipe', 'expert'), may hold values from -0.0625 to 0.0625
- w_router: bfloat16 [8, 3072, 4], P('pipe'), may hold values from -0.109375 to 0.109375
- norm_gain: float32 [8, 3072], P('pipe'), may hold values from 0.25 to 1.75
- route_ids: int32 [8, 4, 64, 2], P('pipe'), may hold values from 0 to 3, all different within a row; in each aligned block of 4 rows (0 to 3, 4 to 7, ..., all dimensions but the last counted through in order) at most 3 rows name the same one
Outputs:
- probes: bfloat16 [8, 4, 64, 3072], P('pipe', None, 'expert')
The draws below stay inside these ranges and needn't reach their ends.
Inputs may be any that keep to these rules, and one draw needn't show every extreme that they name: `route_ids`: the two ids of a token differ. Among the 4 tokens of one index of expert in one layer and micro-batch, no expert is named more than 3 times, and in some such block one expert is named exactly 3 times.
All inputs are finite; a program needn't handle non-finite values.
Results may differ from the reference program's by a relative error of at most 0.029.
Values may be sent and summed in bfloat16 or wider, within the bound.
No kernel may reach another device: no remote copies, remote signals or barrier semaphores. Data moves between devices by JAX's collectives and lax.ppermute only.
A program may use at most 128 MiB of HBM per device.

```python
import math
import jax
import jax.numpy as jnp
import numpy as np
from jax import lax

D = 3072
FF = 8192
EXPERTS = 4
MICRO = 4
TOK_DEV = 4
CAP = 3
TOKENS = 64
LAYERS = 8
N_EXPERT = 16


def steps_of(key, dims, shards, smallest, high):
    def one(position, parts):
        heights = jax.random.uniform(jax.random.fold_in(jax.random.fold_in(key, 6), position), (parts,), jnp.float32, smallest / len(shards), high / len(shards))
        return jnp.repeat(jnp.exp(heights), dims[position] // parts).reshape((-1,) + (1,) * (len(dims) - position - 1))

    factor_of = one(*shards[0])
    for cut in shards[1:]:
        factor_of = factor_of * one(*cut)
    return factor_of


def assign_block(key, own, number, rows, number_of, top, most, lean):
    order = jax.random.permutation(key, number_of)
    packed, common = shares(number_of, rows * top, most, lean, True), shares(number_of, rows * top, most, lean, False)
    places = jnp.arange(number_of)

    def named(lengths, turn):
        used = int((lengths > 0).sum())
        fixed = max(1, used // 4)
        moved = fixed + (places - fixed + turn * (used - fixed)) % max(1, number_of - fixed)
        return jnp.zeros((number_of,), jnp.int32).at[order[jnp.where(places < fixed, places, moved)]].set(jnp.asarray(lengths, jnp.int32))

    lengths = jnp.where(number % 4 == 0, named(packed, number // 4), named(common, number - number // 4 - 1))
    mixed = jax.random.permutation(jax.random.fold_in(own, 3), number_of)
    donor, taker = mixed[0:number_of // 2 * 2:2], mixed[1:number_of // 2 * 2:2]
    room = jnp.minimum(lengths[donor] - 1, most - lengths[taker]) // 2
    room = jnp.where((donor == order[0]) | (taker == order[0]) | (lengths[taker] == 0), 0, jnp.maximum(room, 0))
    moved = jax.random.randint(jax.random.fold_in(own, 4), (number_of // 2,), 0, 1 << 20) % (room + 1)
    lengths = lengths.at[donor].add(-moved).at[taker].add(moved)
    items = jnp.searchsorted(jnp.cumsum(lengths), jnp.arange(rows * top), side="right").astype(jnp.int32)
    grid = items.reshape(top, rows).T
    grid = grid[jax.random.permutation(jax.random.fold_in(own, 1), rows)]
    turn = jax.random.randint(jax.random.fold_in(own, 2), (rows, 1), 0, top)
    return jnp.take_along_axis(grid, (jnp.arange(top)[None, :] + turn) % top, axis=1)


def shares(number_of, total, most, slope, full):
    portions = [(1 << 20) // math.isqrt(grade ** slope) + 1 for grade in range(1, number_of + 1)]
    largest = most if full else min(most, max(-(-total // number_of), total * portions[0] // sum(portions)))
    least = 1 if total - largest >= number_of - 1 else 0
    holding, surplus = [largest] + [least] * (number_of - 1), total - largest - least * (number_of - 1)
    while surplus > 0:
        free = [i for i in range(1, number_of) if holding[i] < largest] or [i for i in range(1, number_of) if holding[i] < most]
        whole, left = sum([portions[i] for i in free]), surplus
        for i in free:
            more = min(most - holding[i], max(1, left * portions[i] // whole), surplus)
            holding[i] = holding[i] + more
            surplus = surplus - more
    return np.array(holding)


def bell_draw(key, shape, deviation, bound, cuts=(), kind=jnp.bfloat16):
    array = deviation * jax.random.normal(key, shape, jnp.float32)
    if cuts:
        array = array * steps_of(key, shape, cuts, -0.22, 0.18)
    return jnp.clip(array, -bound, bound).astype(kind)


def setup_inputs(seed: int = 0) -> dict:
    key_list = jax.random.split(jax.random.key(seed), 8)
    tokens = bell_draw(key_list[0], (MICRO, TOKENS, D), 1.0, 6.0, ((1, 16),))
    tangent = bell_draw(key_list[1], (MICRO, TOKENS, D), 1.0, 6.0, ((1, 16),))
    w_up = bell_draw(key_list[2], (LAYERS, D, EXPERTS * FF), D ** -0.5, 0.109375, ((0, 8), (2, 16)))
    w_down = bell_draw(key_list[3], (LAYERS, EXPERTS * FF, D), FF ** -0.5, 0.0625, ((0, 8), (1, 16)))
    w_router = bell_draw(key_list[4], (LAYERS, D, EXPERTS), D ** -0.5, 0.109375, ((0, 8),))
    norm_gain = jnp.clip(1.0 + 0.15 * jax.random.normal(key_list[5], (LAYERS, D), jnp.float32), 0.25, 1.75)
    route_ids_keys = jax.random.split(jax.random.fold_in(key_list[6], 1), LAYERS * MICRO * TOKENS // TOK_DEV)
    route_ids_turns = jax.random.permutation(jax.random.fold_in(key_list[6], 3), LAYERS * MICRO * TOKENS // TOK_DEV)
    route_ids = jax.vmap(lambda own, number: assign_block(jax.random.fold_in(key_list[6], 2), own, number, TOK_DEV, EXPERTS, 2, CAP, 2))(route_ids_keys, route_ids_turns).reshape((LAYERS, MICRO, TOKENS, 2))
    return {"tokens": tokens, "tangent": tangent, "w_up": w_up, "w_down": w_down, "w_router": w_router, "norm_gain": norm_gain, "route_ids": route_ids}


norm_eps = 1e-05

def slot_rows(id_pairs, tok_width, capacity, expert_total):
    tok_count = id_pairs.shape[0]
    expert_range = jnp.arange(expert_total, dtype=jnp.int32)
    picked = (id_pairs[:, :, None] == expert_range).astype(jnp.int32)
    counts = lax.optimization_barrier(jnp.sum(picked, axis=1)).reshape(tok_count // tok_width, tok_width, expert_total)
    before = (jnp.cumsum(counts, axis=1) - counts).reshape(tok_count, expert_total)
    slot_index = lax.optimization_barrier(jnp.sum(picked * before[:, None, :], axis=2))
    source = (jnp.arange(tok_count, dtype=jnp.int32) // tok_width)[:, None]
    return (source * capacity + slot_index).astype(jnp.int32)

def norm_pair(inputs, tangents, norm_row):
    wide_in = inputs.astype(jnp.float32)
    wide_tan = tangents.astype(jnp.float32)
    row_scale = lax.rsqrt(lax.optimization_barrier(jnp.mean(wide_in * wide_in, axis=-1, keepdims=True)) + norm_eps)
    moment = lax.optimization_barrier(jnp.mean(wide_in * wide_tan, axis=-1, keepdims=True))
    normed = (wide_in * row_scale * norm_row).astype(jnp.bfloat16)
    tangent_normed = (norm_row * (wide_tan * row_scale - wide_in * row_scale ** 3 * moment)).astype(jnp.bfloat16)
    return (row_scale, normed, tangent_normed)

def norm_back(inputs, row_scale, norm_row, cotangent, back_normed):
    wide_in = inputs.astype(jnp.float32)
    weighted = norm_row * back_normed
    moment = lax.optimization_barrier(jnp.mean(wide_in * weighted, axis=-1, keepdims=True))
    result = cotangent.astype(jnp.float32) + row_scale * weighted - wide_in * row_scale ** 3 * moment
    return result.astype(jnp.bfloat16)

def gate_pair(normed, tangent_normed, id_pairs, router, expert_total):
    tok_count = normed.shape[0]
    logits = jnp.dot(jnp.concatenate([normed, tangent_normed], axis=0), router, preferred_element_type=jnp.float32)
    expert_range = jnp.arange(expert_total, dtype=jnp.int32)
    contrast = (id_pairs[:, 0:1] == expert_range).astype(jnp.float32) - (id_pairs[:, 1:2] == expert_range).astype(jnp.float32)
    margin = lax.optimization_barrier(jnp.sum(logits[:tok_count] * contrast, axis=1))
    tangent_margin = lax.optimization_barrier(jnp.sum(logits[tok_count:] * contrast, axis=1))
    first_gate = jax.nn.sigmoid(margin)
    gate_vals = jnp.stack([first_gate, 1.0 - first_gate], axis=1)
    first_move = first_gate * (1.0 - first_gate) * tangent_margin
    gate_moves = jnp.stack([first_move, -first_move], axis=1)
    return (gate_vals, gate_moves)

def expert_pair(rows_in, tangent_rows, w_in, w_out):
    row_count = rows_in.shape[0]
    pre_all = jnp.dot(jnp.concatenate([rows_in, tangent_rows], axis=0), w_in, preferred_element_type=jnp.float32)
    pre_act = pre_all[:row_count]
    tangent_pre = pre_all[row_count:]
    logistic = jax.nn.sigmoid(pre_act)
    hidden = (pre_act * logistic).astype(jnp.bfloat16)
    derivative = logistic * (1.0 + pre_act * (1.0 - logistic))
    tangent_hidden = (derivative * tangent_pre).astype(jnp.bfloat16)
    outputs = jnp.dot(jnp.concatenate([hidden, tangent_hidden], axis=0), w_out, preferred_element_type=jnp.float32)
    return (outputs[:row_count], outputs[row_count:], derivative)

def reference(tokens, tangent, w_up, w_down, w_router, norm_gain, route_ids):
    flat_total = MICRO * N_EXPERT * CAP
    token_total = MICRO * TOKENS
    micro_base = (jnp.arange(MICRO, dtype=jnp.int32) * (N_EXPERT * CAP))[:, None, None]
    expert_range = jnp.arange(EXPERTS, dtype=jnp.int32)
    inputs = tokens.reshape(token_total, D)
    tangents = tangent.reshape(token_total, D)
    history = []
    for layer_idx in range(LAYERS):
        id_grid = route_ids[layer_idx]
        rows_grid = jax.vmap(lambda id_block: slot_rows(id_block, TOK_DEV, CAP, EXPERTS))(id_grid)
        positions = (rows_grid + micro_base).reshape(token_total, 2).astype(jnp.int32)
        id_pairs = id_grid.reshape(token_total, 2).astype(jnp.int32)
        row_scale, normed, tangent_normed = norm_pair(inputs, tangents, norm_gain[layer_idx])
        gate_vals, gate_moves = gate_pair(normed, tangent_normed, id_pairs, w_router[layer_idx], EXPERTS)
        both_rows = jnp.stack([normed, tangent_normed], axis=1)
        buffer = jnp.zeros((EXPERTS, flat_total, 2, D), jnp.bfloat16)
        for pick_idx in range(2):
            buffer = buffer.at[id_pairs[:, pick_idx], positions[:, pick_idx]].set(both_rows)
        w_in_all = w_up[layer_idx]
        w_out_all = w_down[layer_idx]

        def one_expert(expert_idx):
            w_in = lax.dynamic_slice_in_dim(w_in_all, expert_idx * FF, FF, 1)
            w_out = lax.dynamic_slice_in_dim(w_out_all, expert_idx * FF, FF, 0)
            block_rows = lax.dynamic_index_in_dim(buffer, expert_idx, 0, keepdims=False)
            return expert_pair(block_rows[:, 0], block_rows[:, 1], w_in, w_out)
        main_out, tangent_out, derivative = lax.map(one_expert, expert_range)
        expert_vals = jnp.stack([main_out[id_pairs[:, pick_idx], positions[:, pick_idx]] for pick_idx in range(2)], axis=1)
        tangent_vals = jnp.stack([tangent_out[id_pairs[:, pick_idx], positions[:, pick_idx]] for pick_idx in range(2)], axis=1)
        main_sum = lax.optimization_barrier(jnp.sum(gate_vals[:, :, None] * expert_vals, axis=1))
        tangent_sum = lax.optimization_barrier(jnp.sum(gate_moves[:, :, None] * expert_vals + gate_vals[:, :, None] * tangent_vals, axis=1))
        history.append((inputs, row_scale, gate_vals, expert_vals, derivative, id_pairs, positions))
        inputs = (inputs.astype(jnp.float32) + main_sum).astype(jnp.bfloat16)
        tangents = (tangents.astype(jnp.float32) + tangent_sum).astype(jnp.bfloat16)
    cotangent = tangents
    probe_list = []
    for layer_idx in reversed(range(LAYERS)):
        layer_in, row_scale, gate_vals, expert_vals, derivative, id_pairs, positions = history[layer_idx]
        buffer = jnp.zeros((EXPERTS, flat_total, D), jnp.bfloat16)
        for pick_idx in range(2):
            buffer = buffer.at[id_pairs[:, pick_idx], positions[:, pick_idx]].set(cotangent)
        w_in_all = w_up[layer_idx]
        w_out_all = w_down[layer_idx]

        def one_back(expert_idx):
            w_in = lax.dynamic_slice_in_dim(w_in_all, expert_idx * FF, FF, 1)
            w_out = lax.dynamic_slice_in_dim(w_out_all, expert_idx * FF, FF, 0)
            rows_in = lax.dynamic_index_in_dim(buffer, expert_idx, 0, keepdims=False)
            slope_in = lax.dynamic_index_in_dim(derivative, expert_idx, 0, keepdims=False)
            back_hidden = (slope_in * jnp.dot(rows_in, w_out.T, preferred_element_type=jnp.float32)).astype(jnp.bfloat16)
            return jnp.dot(back_hidden, w_in.T, preferred_element_type=jnp.float32)
        back_all = lax.map(one_back, expert_range)
        back_tok = jnp.stack([back_all[id_pairs[:, pick_idx], positions[:, pick_idx]] for pick_idx in range(2)], axis=1)
        back_sum = lax.optimization_barrier(jnp.sum(gate_vals[:, :, None] * back_tok, axis=1))
        gate_pull = lax.optimization_barrier(jnp.sum(cotangent.astype(jnp.float32)[:, None, :] * expert_vals, axis=2))
        gate_grad = gate_vals[:, 0] * gate_vals[:, 1] * (gate_pull[:, 0] - gate_pull[:, 1])
        router_rows = w_router[layer_idx].T.astype(jnp.float32)
        router_gap = router_rows[id_pairs[:, 0]] - router_rows[id_pairs[:, 1]]
        back_normed = back_sum + gate_grad[:, None] * router_gap
        cotangent = norm_back(layer_in, row_scale, norm_gain[layer_idx], cotangent, back_normed)
        probe_list.append(cotangent.reshape(MICRO, TOKENS, D))
    return jnp.stack(probe_list[::-1])
```

```python
import jax
import jax.numpy as jnp
from jax import lax
from jax.experimental import pallas as pl
from jax.experimental.pallas import tpu as pltpu
from jax.sharding import PartitionSpec as P

EXPERTS = 4
SIDE = 4
LANES = 128
TILE = 512
CHUNK = 512
KERNEL_VMEM = 36 * 2**20

norm_eps = 1e-05
BF = jnp.bfloat16
F32 = jnp.float32


def z_send(block, distance):
    route = [(4 * y + z, 4 * y + (z + distance) % 4) for y in range(4) for z in range(4)]
    return lax.ppermute(block, "expert", route)


def y_send(block, distance):
    route = [(4 * y + z, 4 * ((y + distance) % 4) + z) for y in range(4) for z in range(4)]
    return lax.ppermute(block, "expert", route)


def pipe_send(block, hops, distance):
    route = [
        (16 * p + 4 * y + z, 16 * q + 4 * y + (z + distance) % 4)
        for p, q in hops
        for y in range(4)
        for z in range(4)
    ]
    return lax.ppermute(block, ("pipe", "expert"), route)


def pipe_gather(block, hops):
    return [pipe_send(block, hops, d) for d in range(SIDE)]


FORWARD_HOPS = (((1, 2), (3, 4), (5, 6)), ((0, 1), (2, 3), (4, 5), (6, 7)))
FIRST_HOPS = (((7, 0), (1, 2), (3, 4), (5, 6)), FORWARD_HOPS[1])
BACKWARD_HOPS = (((7, 7), (6, 5), (4, 3), (2, 1)), ((7, 6), (5, 4), (3, 2), (1, 0)))


def forward_kernel(idx_ref, a0, a1, a2, a3, c_ref, gain_ref, router_ref, up_hbm, down_hbm,
                   x_in, der_in, hid_in, gate_in, o0, o1, o2, o3, x_store, der_store, hid_store,
                   gate_store, nrm, hid, der, gates, up_ref, down_ref, sems, up_sems, down_sems):
    rows = a0.shape[1]
    total = SIDE * rows
    width, ff = up_ref.shape
    micro_idx = idx_ref[0]

    def up_copy(j):
        span = pl.ds(pl.multiple_of(j * CHUNK, CHUNK), CHUNK)
        return pltpu.make_async_copy(up_hbm.at[:, span], up_ref.at[:, span], up_sems.at[j])

    def down_copy(j):
        span = pl.ds(pl.multiple_of(j * CHUNK, CHUNK), CHUNK)
        return pltpu.make_async_copy(down_hbm.at[:, span], down_ref.at[:, span], down_sems.at[j])

    @pl.loop(0, ff // CHUNK)
    def _(j):
        up_copy(j).start()

    @pl.loop(0, width // CHUNK)
    def _(j):
        down_copy(j).start()

    saves = [
        pltpu.make_async_copy(a0.at[0], x_store.at[micro_idx], sems.at[0]),
        pltpu.make_async_copy(der, der_store.at[micro_idx], sems.at[1]),
        pltpu.make_async_copy(hid.at[pl.ds(0, total)], hid_store.at[micro_idx], sems.at[2]),
        pltpu.make_async_copy(gates, gate_store.at[micro_idx], sems.at[3]),
    ]

    saves[0].start()
    gain = gain_ref[...]
    for d, a in enumerate((a0, a1, a2, a3)):
        x = a[0].astype(F32)
        t = a[1].astype(F32)
        scale = lax.rsqrt(jnp.mean(x * x, axis=-1, keepdims=True) + norm_eps)
        moment = jnp.mean(x * t, axis=-1, keepdims=True)
        nrm[pl.ds(d * rows, rows), :] = (x * scale * gain).astype(BF)
        nrm[pl.ds(total + d * rows, rows), :] = (
            gain * (t * scale - x * (scale * scale * scale) * moment)
        ).astype(BF)
    logits = jnp.dot(nrm[...], router_ref[...], preferred_element_type=F32)
    contrast = c_ref[micro_idx]
    lane = lax.broadcasted_iota(jnp.int32, contrast.shape, 1)
    side = jnp.sum(jnp.where(lane == idx_ref[1], contrast, 0.0), axis=1, keepdims=True)
    margin = jnp.sum(logits[:total] * contrast, axis=1, keepdims=True)
    move = jnp.sum(logits[total:] * contrast, axis=1, keepdims=True)
    first = jax.nn.sigmoid(margin)
    slope = first * (1.0 - first)
    gate = jnp.where(side > 0.5, first, jnp.where(side < -0.5, 1.0 - first, 0.0))
    gates[0] = jnp.broadcast_to(gate, contrast.shape)
    gates[1] = jnp.broadcast_to(side * slope, contrast.shape)
    gates[2] = jnp.broadcast_to(side * slope * move, contrast.shape)
    saves[3].start()

    @pl.loop(0, ff // CHUNK)
    def _(chunk):
        up_copy(chunk).wait()

        @pl.loop(0, CHUNK // TILE)
        def _(tile):
            span = pl.ds(pl.multiple_of(chunk * CHUNK + tile * TILE, TILE), TILE)
            pre_all = jnp.dot(nrm[...], up_ref[:, span], preferred_element_type=F32)
            pre = pre_all[:total]
            logistic = jax.nn.sigmoid(pre)
            derivative = logistic * (1.0 + pre * (1.0 - logistic))
            der[:, span] = derivative
            hid[pl.ds(0, total), span] = (pre * logistic).astype(BF)
            hid[pl.ds(total, total), span] = (derivative * pre_all[total:]).astype(BF)

    saves[1].start()
    saves[2].start()
    gate = gates[0, :, 0:1]
    shift = gates[2, :, 0:1]

    @pl.loop(0, width // CHUNK)
    def _(chunk):
        down_copy(chunk).wait()

        @pl.loop(0, CHUNK // TILE)
        def _(tile):
            span = pl.ds(pl.multiple_of(chunk * CHUNK + tile * TILE, TILE), TILE)
            both = jnp.dot(hid[...], down_ref[:, span], preferred_element_type=F32)
            main = (gate * both[:total]).astype(BF)
            moved = (shift * both[:total] + gate * both[total:]).astype(BF)
            for d, o in enumerate((o0, o1, o2, o3)):
                o[0, :, span] = main[d * rows:(d + 1) * rows]
                o[1, :, span] = moved[d * rows:(d + 1) * rows]

    for save in saves:
        save.wait()


def backward_kernel(idx_ref, b0, b1, b2, b3, c_ref, router_ref, up_hbm, down_hbm, der_store,
                    hid_store, gate_store, o0, o1, o2, o3, cot, back_hid, hid, der, gates,
                    up_ref, down_ref, sems, up_sems, down_sems):
    rows = b0.shape[0]
    total = SIDE * rows
    width, ff = up_ref.shape
    micro_idx = idx_ref[0]

    def up_copy(j):
        span = pl.ds(pl.multiple_of(j * CHUNK, CHUNK), CHUNK)
        return pltpu.make_async_copy(up_hbm.at[span, :], up_ref.at[span, :], up_sems.at[j])

    def down_copy(j):
        span = pl.ds(pl.multiple_of(j * CHUNK, CHUNK), CHUNK)
        return pltpu.make_async_copy(down_hbm.at[span, :], down_ref.at[span, :], down_sems.at[j])

    loads = [
        pltpu.make_async_copy(der_store.at[micro_idx], der, sems.at[0]),
        pltpu.make_async_copy(hid_store.at[micro_idx], hid, sems.at[1]),
        pltpu.make_async_copy(gate_store.at[micro_idx], gates, sems.at[2]),
    ]

    for load in loads:
        load.start()

    @pl.loop(0, ff // CHUNK)
    def _(j):
        down_copy(j).start()

    @pl.loop(0, width // CHUNK)
    def _(j):
        up_copy(j).start()

    @pl.loop(0, width // CHUNK)
    def _(j):
        span = pl.ds(pl.multiple_of(j * CHUNK, CHUNK), CHUNK)
        part = jnp.concatenate([b[:, span] for b in (b0, b1, b2, b3)] * 2, axis=0)
        cot[span, :] = part.T
    for load in loads:
        load.wait()

    def hidden_step(chunk, pull):
        down_copy(chunk).wait()

        def tile_step(tile, pull):
            span = pl.ds(pl.multiple_of(chunk * CHUNK + tile * TILE, TILE), TILE)
            back = jnp.dot(down_ref[span, :], cot[...], preferred_element_type=F32)
            slope = der[:, span]
            value = hid[:, span].astype(F32)
            slope = jnp.concatenate([slope, slope], axis=0).T
            value = jnp.concatenate([value, value], axis=0).T
            back_hid[span, :] = (slope * back).astype(BF)
            return pull + jnp.sum(back * value, axis=0, keepdims=True)

        return lax.fori_loop(0, CHUNK // TILE, tile_step, pull)

    pull = lax.fori_loop(0, ff // CHUNK, hidden_step, jnp.zeros((1, 2 * total), F32))
    pull = jnp.broadcast_to(pull, (LANES, 2 * total)).T[:total, 0:1]
    gate = gates[0, :, 0:1]
    grad = gates[1, :, 0:1] * pull
    contrast = c_ref[micro_idx].astype(BF)

    @pl.loop(0, width // CHUNK)
    def _(chunk):
        up_copy(chunk).wait()

        @pl.loop(0, CHUNK // TILE)
        def _(tile):
            span = pl.ds(pl.multiple_of(chunk * CHUNK + tile * TILE, TILE), TILE)
            back = jnp.dot(up_ref[span, :], back_hid[...], preferred_element_type=F32).T[:total]
            gap = lax.dot_general(
                contrast, router_ref[span, :], (((1,), (1,)), ((), ())), preferred_element_type=F32
            )
            part = (gate * back + grad * gap).astype(BF)
            for d, o in enumerate((o0, o1, o2, o3)):
                o[:, span] = part[d * rows:(d + 1) * rows]


SMEM_SPEC = pl.BlockSpec(memory_space=pltpu.SMEM)
VMEM_SPEC = pl.BlockSpec(memory_space=pltpu.VMEM)
ANY_SPEC = pl.BlockSpec(memory_space=pl.ANY)


def run_forward(idx, blocks, contrast, gain, router, w_in, w_out, stores):
    _, rows, width = blocks[0].shape
    ff = w_in.shape[1]
    total = SIDE * rows
    block = jax.ShapeDtypeStruct((2, rows, width), BF)
    out = pl.pallas_call(
        forward_kernel,
        out_shape=(block,) * 4 + tuple(jax.ShapeDtypeStruct(s.shape, s.dtype) for s in stores),
        in_specs=[SMEM_SPEC] + [VMEM_SPEC] * 7 + [ANY_SPEC] * 6,
        out_specs=[VMEM_SPEC] * 4 + [ANY_SPEC] * 4,
        scratch_shapes=[
            pltpu.VMEM((2 * total, width), BF),
            pltpu.VMEM((2 * total, ff), BF),
            pltpu.VMEM((total, ff), F32),
            pltpu.VMEM((3, total, LANES), F32),
            pltpu.VMEM(w_in.shape, BF),
            pltpu.VMEM(w_out.shape, BF),
            pltpu.SemaphoreType.DMA((4,)),
            pltpu.SemaphoreType.DMA((ff // CHUNK,)),
            pltpu.SemaphoreType.DMA((width // CHUNK,)),
        ],
        input_output_aliases={10: 4, 11: 5, 12: 6, 13: 7},
        compiler_params=pltpu.CompilerParams(vmem_limit_bytes=KERNEL_VMEM),
        name="forward_layer",
    )(idx, *blocks, contrast, gain, router, w_in, w_out, *stores)
    return out[:4], tuple(out[4:])


def run_backward(idx, blocks, contrast, router, w_in, w_out, stores):
    rows, width = blocks[0].shape
    ff = w_in.shape[1]
    total = SIDE * rows
    block = jax.ShapeDtypeStruct((rows, width), BF)
    return pl.pallas_call(
        backward_kernel,
        out_shape=(block,) * 4,
        in_specs=[SMEM_SPEC] + [VMEM_SPEC] * 6 + [ANY_SPEC] * 5,
        out_specs=[VMEM_SPEC] * 4,
        scratch_shapes=[
            pltpu.VMEM((width, 2 * total), BF),
            pltpu.VMEM((ff, 2 * total), BF),
            pltpu.VMEM((total, ff), BF),
            pltpu.VMEM((total, ff), F32),
            pltpu.VMEM((3, total, LANES), F32),
            pltpu.VMEM(w_in.shape, BF),
            pltpu.VMEM(w_out.shape, BF),
            pltpu.SemaphoreType.DMA((3,)),
            pltpu.SemaphoreType.DMA((width // CHUNK,)),
            pltpu.SemaphoreType.DMA((ff // CHUNK,)),
        ],
        compiler_params=pltpu.CompilerParams(vmem_limit_bytes=KERNEL_VMEM),
        name="backward_layer",
    )(idx, *blocks, contrast, router, w_in, w_out, *stores[1:])


def unset(*leaves):
    return pl.pallas_call(
        lambda *refs: None,
        out_shape=tuple(jax.ShapeDtypeStruct(shape, kind) for shape, kind in leaves),
        out_specs=(ANY_SPEC,) * len(leaves),
        name="unset",
    )()


def shards(tokens, tangent, w_up, w_down, w_router, norm_gain, route_ids):
    micro_count, tok_width, width = tokens.shape
    pipe_count = lax.axis_size("pipe")
    section = lax.axis_index("pipe")
    rank = lax.axis_index("expert")
    expert_y = rank // SIDE
    place_z = rank % SIDE
    w_in = w_up[0]
    w_out = w_down[0]
    gain = norm_gain
    router = jnp.pad(w_router[0], ((0, 0), (0, LANES - EXPERTS)))
    ff = w_in.shape[1]
    rows = SIDE * tok_width
    total = SIDE * rows

    ids = route_ids[0].reshape(micro_count, SIDE, SIDE, tok_width, 2)
    ids = ids.transpose(0, 2, 1, 3, 4).reshape(micro_count, SIDE, rows, 2)
    relative = (place_z - jnp.arange(SIDE)) % SIDE
    ids = jnp.take(ids, relative, axis=1).reshape(micro_count, total, 2)
    lane = jnp.arange(LANES, dtype=jnp.int32)
    contrast = (ids[:, :, 0:1] == lane).astype(F32) - (ids[:, :, 1:2] == lane).astype(F32)
    contrast, router = lax.optimization_barrier((contrast, router))

    start = jnp.stack([tokens, tangent], axis=1)
    groups = [[SIDE * y + z for y in range(SIDE)] for z in range(SIDE)]
    start = lax.all_gather(start, "expert", axis=2, tiled=True, axis_index_groups=groups)

    def reduce_all(parts):
        got = [z_send(parts[4 - d], d) for d in (1, 2, 3)]
        mine = parts[0].astype(F32) + got[0].astype(F32) + got[1].astype(F32) + got[2].astype(F32)
        mine = mine.astype(BF)
        got = [y_send(mine, d) for d in (1, 2, 3)]
        return mine.astype(F32) + got[0].astype(F32) + got[1].astype(F32) + got[2].astype(F32)

    def make_idx(micro_idx):
        return jnp.stack([micro_idx, expert_y]).astype(jnp.int32)

    def plan(step):
        micro_idx = step // 2
        active = (step >= 0) & (step % 2 == 0) & (micro_idx < micro_count)
        return active, jnp.clip(micro_idx, 0, micro_count - 1)

    def forward_plan(tick):
        return plan(tick - section)

    def backward_plan(tick):
        return plan(tick - (2 * pipe_count - 1 - section))

    def fresh(tick):
        micro_idx = jnp.clip((tick + 1) // 2, 0, micro_count - 1)
        return lax.dynamic_index_in_dim(start, micro_idx, 0, keepdims=False)

    def forward_half(tick, blocks, back, stores, first):
        active, micro_idx = forward_plan(tick)
        last = section == pipe_count - 1

        def run(blocks, back, stores):
            parts, stores = run_forward(
                make_idx(micro_idx), blocks, contrast, gain, router, w_in, w_out, stores
            )
            out = (blocks[0].astype(F32) + reduce_all(parts)).astype(BF)
            return out, jnp.where(last, out[1], back), stores

        def rest(blocks, back, stores):
            out = jnp.where(last, fresh(tick), blocks[0]) if first else blocks[0]
            return out, back, stores

        return lax.cond(active, run, rest, blocks, back, stores)

    def store_probe(tick, result, probe_store):
        active, micro_idx = backward_plan(tick)
        write_idx = jnp.where(active, micro_idx, micro_count)
        return lax.dynamic_update_index_in_dim(probe_store, result, write_idx, 0)

    def backward_half(tick, blocks, stores):
        active, micro_idx = backward_plan(tick)

        def run(blocks, stores):
            parts = run_backward(
                make_idx(micro_idx), blocks, contrast, router, w_in, w_out, stores
            )
            back_normed = reduce_all(parts)
            wide = lax.dynamic_index_in_dim(stores[0], micro_idx, 0, keepdims=False).astype(F32)
            scale = lax.rsqrt(jnp.mean(wide * wide, axis=-1, keepdims=True) + norm_eps)
            weighted = gain * back_normed
            moment = jnp.mean(wide * weighted, axis=-1, keepdims=True)
            moved = blocks[0].astype(F32) + scale * weighted - wide * scale**3 * moment
            return moved.astype(BF)

        return lax.cond(active, run, lambda blocks, stores: blocks[0], blocks, stores)

    *stores, probe_store = unset(
        ((10 * micro_count, rows, width), BF),
        ((2 * micro_count, total, ff), F32),
        ((4 * micro_count, total, ff), BF),
        ((12 * micro_count, 3, total, LANES), F32),
        ((10 * micro_count, rows, width), BF),
    )
    stores = tuple(stores)
    back = jnp.zeros((rows, width), BF)

    def forward_ticks(pair_idx, state):
        out, back, stores = state
        for parity in range(2):
            tick = 2 * pair_idx + parity
            blocks = pipe_gather(out, FIRST_HOPS[parity])
            out, back, stores = forward_half(tick, blocks, back, stores, True)
        return out, back, stores

    def both_ticks(pair_idx, state):
        out, back, stores, probe_store = state
        for parity in range(2):
            tick = 2 * pair_idx + parity
            back_blocks = pipe_gather(back, BACKWARD_HOPS[parity])
            blocks = pipe_gather(out, FORWARD_HOPS[parity])
            probe_store = store_probe(tick - 1, back, probe_store)
            back = backward_half(tick, back_blocks, stores)
            out, back, stores = forward_half(tick, blocks, back, stores, False)
        return out, back, stores, probe_store

    def backward_ticks(pair_idx, state):
        back, probe_store = state
        for parity in range(2):
            tick = 2 * pair_idx + parity
            back_blocks = pipe_gather(back, BACKWARD_HOPS[parity])
            probe_store = store_probe(tick - 1, back, probe_store)
            back = backward_half(tick, back_blocks, stores)
        return back, probe_store

    lead = pipe_count // 2
    turn = lead + micro_count - 1
    out, back, stores = lax.fori_loop(0, lead, forward_ticks, (start[0], back, stores))
    out, back, stores, probe_store = lax.fori_loop(
        lead, turn, both_ticks, (out, back, stores, probe_store)
    )
    back, probe_store = lax.fori_loop(
        turn, pipe_count + micro_count - 1, backward_ticks, (back, probe_store)
    )
    probe_store = store_probe(2 * pipe_count + 2 * micro_count - 3, back, probe_store)
    probes = probe_store[:micro_count].reshape(micro_count, SIDE, tok_width, width)
    probes = lax.dynamic_index_in_dim(probes, expert_y, 1, keepdims=False)
    return probes[None]


def solution(mesh):
    in_specs = (
        P(None, "expert", None),
        P(None, "expert", None),
        P("pipe", None, "expert"),
        P("pipe", "expert", None),
        P("pipe", None, None),
        P("pipe", None),
        P("pipe", None, None, None),
    )
    out_specs = P("pipe", None, "expert", None)
    return jax.shard_map(shards, mesh=mesh, in_specs=in_specs, out_specs=out_specs, check_vma=False)
```

```python
import jax
import jax.numpy as jnp
from jax import lax
from jax.experimental import pallas as pl
from jax.experimental.pallas import tpu as pltpu
from jax.sharding import PartitionSpec as P

EXPERTS = 4
SIDE = 4
LANES = 128
TILE = 512
CHUNK = 512
KERNEL_VMEM = 36 * 2**20

norm_eps = 1e-05
BF = jnp.bfloat16
F32 = jnp.float32


def z_send(block, distance):
    route = [(4 * y + z, 4 * y + (z + distance) % 4) for y in range(4) for z in range(4)]
    return lax.ppermute(block, "expert", route)


def y_send(block, distance):
    route = [(4 * y + z, 4 * ((y + distance) % 4) + z) for y in range(4) for z in range(4)]
    return lax.ppermute(block, "expert", route)


def pipe_send(block, hops, distance):
    route = [
        (16 * p + 4 * y + z, 16 * q + 4 * y + (z + distance) % 4)
        for p, q in hops
        for y in range(4)
        for z in range(4)
    ]
    return lax.ppermute(block, ("pipe", "expert"), route)


def pipe_gather(block, hops):
    sent = {d: pipe_send(block, hops, d) for d in (2, 1, 3, 0)}
    return [sent[d] for d in range(SIDE)]


FORWARD_HOPS = (((1, 2), (3, 4), (5, 6)), ((0, 1), (2, 3), (4, 5), (6, 7)))
FIRST_HOPS = (((7, 0), (1, 2), (3, 4), (5, 6)), FORWARD_HOPS[1])
BACKWARD_HOPS = (((7, 7), (6, 5), (4, 3), (2, 1)), ((7, 6), (5, 4), (3, 2), (1, 0)))


def forward_kernel(idx_ref, a0, a1, a2, a3, c_ref, gain_ref, router_ref, up_hbm, down_hbm,
                   x_in, der_in, hid_in, gate_in, o0, o1, o2, o3, x_store, der_store, hid_store,
                   gate_store, nrm, hid, der, gates, up_ref, down_ref, sems, up_sems, down_sems):
    rows = a0.shape[1]
    total = SIDE * rows
    width, ff = up_ref.shape
    micro_idx = idx_ref[0]

    def up_copy(j):
        span = pl.ds(pl.multiple_of(j * CHUNK, CHUNK), CHUNK)
        return pltpu.make_async_copy(up_hbm.at[:, span], up_ref.at[:, span], up_sems.at[j])

    def down_copy(j):
        span = pl.ds(pl.multiple_of(j * CHUNK, CHUNK), CHUNK)
        return pltpu.make_async_copy(down_hbm.at[:, span], down_ref.at[:, span], down_sems.at[j])

    @pl.loop(0, ff // CHUNK)
    def _(j):
        up_copy(j).start()

    @pl.loop(0, width // CHUNK)
    def _(j):
        down_copy(j).start()

    saves = [
        pltpu.make_async_copy(a0.at[0], x_store.at[micro_idx], sems.at[0]),
        pltpu.make_async_copy(der, der_store.at[micro_idx], sems.at[1]),
        pltpu.make_async_copy(hid.at[pl.ds(0, total)], hid_store.at[micro_idx], sems.at[2]),
        pltpu.make_async_copy(gates, gate_store.at[micro_idx], sems.at[3]),
    ]

    saves[0].start()
    gain = gain_ref[...]
    for d, a in enumerate((a0, a1, a2, a3)):
        x = a[0].astype(F32)
        t = a[1].astype(F32)
        scale = lax.rsqrt(jnp.mean(x * x, axis=-1, keepdims=True) + norm_eps)
        moment = jnp.mean(x * t, axis=-1, keepdims=True)
        nrm[pl.ds(d * rows, rows), :] = (x * scale * gain).astype(BF)
        nrm[pl.ds(total + d * rows, rows), :] = (
            gain * (t * scale - x * (scale * scale * scale) * moment)
        ).astype(BF)
    logits = jnp.dot(nrm[...], router_ref[...], preferred_element_type=F32)
    contrast = c_ref[micro_idx]
    lane = lax.broadcasted_iota(jnp.int32, contrast.shape, 1)
    side = jnp.sum(jnp.where(lane == idx_ref[1], contrast, 0.0), axis=1, keepdims=True)
    margin = jnp.sum(logits[:total] * contrast, axis=1, keepdims=True)
    move = jnp.sum(logits[total:] * contrast, axis=1, keepdims=True)
    first = jax.nn.sigmoid(margin)
    slope = first * (1.0 - first)
    gate = jnp.where(side > 0.5, first, jnp.where(side < -0.5, 1.0 - first, 0.0))
    gates[0] = jnp.broadcast_to(gate, contrast.shape)
    gates[1] = jnp.broadcast_to(side * slope, contrast.shape)
    gates[2] = jnp.broadcast_to(side * slope * move, contrast.shape)
    saves[3].start()

    @pl.loop(0, ff // CHUNK)
    def _(chunk):
        up_copy(chunk).wait()

        @pl.loop(0, CHUNK // TILE)
        def _(tile):
            span = pl.ds(pl.multiple_of(chunk * CHUNK + tile * TILE, TILE), TILE)
            pre_all = jnp.dot(nrm[...], up_ref[:, span], preferred_element_type=F32)
            pre = pre_all[:total]
            logistic = jax.nn.sigmoid(pre)
            derivative = logistic * (1.0 + pre * (1.0 - logistic))
            der[:, span] = derivative
            hid[pl.ds(0, total), span] = (pre * logistic).astype(BF)
            hid[pl.ds(total, total), span] = (derivative * pre_all[total:]).astype(BF)

    saves[1].start()
    saves[2].start()
    gate = gates[0, :, 0:1]
    shift = gates[2, :, 0:1]

    @pl.loop(0, width // CHUNK)
    def _(chunk):
        down_copy(chunk).wait()

        @pl.loop(0, CHUNK // TILE)
        def _(tile):
            span = pl.ds(pl.multiple_of(chunk * CHUNK + tile * TILE, TILE), TILE)
            both = jnp.dot(hid[...], down_ref[:, span], preferred_element_type=F32)
            main = (gate * both[:total]).astype(BF)
            moved = (shift * both[:total] + gate * both[total:]).astype(BF)
            for d, o in enumerate((o0, o1, o2, o3)):
                o[0, :, span] = main[d * rows:(d + 1) * rows]
                o[1, :, span] = moved[d * rows:(d + 1) * rows]

    for save in saves:
        save.wait()


def backward_kernel(idx_ref, b0, b1, b2, b3, c_ref, router_ref, up_hbm, down_hbm, x_store,
                    der_store, hid_store, gate_store, o0, o1, o2, o3, x_ref, cot, back_hid, hid,
                    der, gates, up_ref, down_ref, sems, up_sems, down_sems):
    rows = b0.shape[0]
    total = SIDE * rows
    width, ff = up_ref.shape
    micro_idx = idx_ref[0]

    def up_copy(j):
        span = pl.ds(pl.multiple_of(j * CHUNK, CHUNK), CHUNK)
        return pltpu.make_async_copy(up_hbm.at[span, :], up_ref.at[span, :], up_sems.at[j])

    def down_copy(j):
        span = pl.ds(pl.multiple_of(j * CHUNK, CHUNK), CHUNK)
        return pltpu.make_async_copy(down_hbm.at[span, :], down_ref.at[span, :], down_sems.at[j])

    loads = [
        pltpu.make_async_copy(der_store.at[micro_idx], der, sems.at[0]),
        pltpu.make_async_copy(hid_store.at[micro_idx], hid, sems.at[1]),
        pltpu.make_async_copy(gate_store.at[micro_idx], gates, sems.at[2]),
        pltpu.make_async_copy(x_store.at[micro_idx], x_ref, sems.at[3]),
    ]

    for load in loads:
        load.start()

    @pl.loop(0, ff // CHUNK)
    def _(j):
        down_copy(j).start()

    @pl.loop(0, width // CHUNK)
    def _(j):
        up_copy(j).start()

    @pl.loop(0, width // CHUNK)
    def _(j):
        span = pl.ds(pl.multiple_of(j * CHUNK, CHUNK), CHUNK)
        part = jnp.concatenate([b[:, span] for b in (b0, b1, b2, b3)] * 2, axis=0)
        cot[span, :] = part.T
    for load in loads:
        load.wait()

    def hidden_step(chunk, pull):
        down_copy(chunk).wait()

        def tile_step(tile, pull):
            span = pl.ds(pl.multiple_of(chunk * CHUNK + tile * TILE, TILE), TILE)
            back = jnp.dot(down_ref[span, :], cot[...], preferred_element_type=F32)
            value = hid[:, span].astype(F32)
            both = jnp.concatenate([der[:, span], value], axis=0).T * back
            back_hid[span, :] = both.astype(BF)
            return pull + jnp.sum(both, axis=0, keepdims=True)

        return lax.fori_loop(0, CHUNK // TILE, tile_step, pull)

    pull = lax.fori_loop(0, ff // CHUNK, hidden_step, jnp.zeros((1, 2 * total), F32))
    pull = jnp.broadcast_to(pull, (LANES, 2 * total)).T[total:, 0:1]
    gate = gates[0, :, 0:1]
    grad = gates[1, :, 0:1] * pull
    contrast = c_ref[micro_idx].astype(BF)

    @pl.loop(0, width // CHUNK)
    def _(chunk):
        up_copy(chunk).wait()

        @pl.loop(0, CHUNK // TILE)
        def _(tile):
            span = pl.ds(pl.multiple_of(chunk * CHUNK + tile * TILE, TILE), TILE)
            back = jnp.dot(up_ref[span, :], back_hid[...], preferred_element_type=F32).T[:total]
            gap = lax.dot_general(
                contrast, router_ref[span, :], (((1,), (1,)), ((), ())), preferred_element_type=F32
            )
            part = (gate * back + grad * gap).astype(BF)
            for d, o in enumerate((o0, o1, o2, o3)):
                o[:, span] = part[d * rows:(d + 1) * rows]


SMEM_SPEC = pl.BlockSpec(memory_space=pltpu.SMEM)
VMEM_SPEC = pl.BlockSpec(memory_space=pltpu.VMEM)
ANY_SPEC = pl.BlockSpec(memory_space=pl.ANY)


def run_forward(idx, blocks, contrast, gain, router, w_in, w_out, stores):
    _, rows, width = blocks[0].shape
    ff = w_in.shape[1]
    total = SIDE * rows
    block = jax.ShapeDtypeStruct((2, rows, width), BF)
    out = pl.pallas_call(
        forward_kernel,
        out_shape=(block,) * 4 + tuple(jax.ShapeDtypeStruct(s.shape, s.dtype) for s in stores),
        in_specs=[SMEM_SPEC] + [VMEM_SPEC] * 7 + [ANY_SPEC] * 6,
        out_specs=[VMEM_SPEC] * 4 + [ANY_SPEC] * 4,
        scratch_shapes=[
            pltpu.VMEM((2 * total, width), BF),
            pltpu.VMEM((2 * total, ff), BF),
            pltpu.VMEM((total, ff), F32),
            pltpu.VMEM((3, total, LANES), F32),
            pltpu.VMEM(w_in.shape, BF),
            pltpu.VMEM(w_out.shape, BF),
            pltpu.SemaphoreType.DMA((4,)),
            pltpu.SemaphoreType.DMA((ff // CHUNK,)),
            pltpu.SemaphoreType.DMA((width // CHUNK,)),
        ],
        input_output_aliases={10: 4, 11: 5, 12: 6, 13: 7},
        compiler_params=pltpu.CompilerParams(vmem_limit_bytes=KERNEL_VMEM),
        name="forward_layer",
    )(idx, *blocks, contrast, gain, router, w_in, w_out, *stores)
    return out[:4], tuple(out[4:])


def run_backward(idx, blocks, contrast, router, w_in, w_out, stores):
    rows, width = blocks[0].shape
    ff = w_in.shape[1]
    total = SIDE * rows
    block = jax.ShapeDtypeStruct((rows, width), BF)
    return pl.pallas_call(
        backward_kernel,
        out_shape=(block,) * 5,
        in_specs=[SMEM_SPEC] + [VMEM_SPEC] * 6 + [ANY_SPEC] * 6,
        out_specs=[VMEM_SPEC] * 5,
        scratch_shapes=[
            pltpu.VMEM((width, 2 * total), BF),
            pltpu.VMEM((ff, 2 * total), BF),
            pltpu.VMEM((total, ff), BF),
            pltpu.VMEM((total, ff), F32),
            pltpu.VMEM((3, total, LANES), F32),
            pltpu.VMEM(w_in.shape, BF),
            pltpu.VMEM(w_out.shape, BF),
            pltpu.SemaphoreType.DMA((4,)),
            pltpu.SemaphoreType.DMA((width // CHUNK,)),
            pltpu.SemaphoreType.DMA((ff // CHUNK,)),
        ],
        compiler_params=pltpu.CompilerParams(vmem_limit_bytes=KERNEL_VMEM),
        name="backward_layer",
    )(idx, *blocks, contrast, router, w_in, w_out, *stores)


def forward_finish(block_ref, m0, m1, m2, m3, out_ref, back_ref):
    moved = m0[...].astype(F32) + m1[...].astype(F32) + m2[...].astype(F32) + m3[...].astype(F32)
    out_ref[...] = (block_ref[...].astype(F32) + moved).astype(BF)
    back_ref[...] = out_ref[1]


def backward_finish(block_ref, x_ref, gain_ref, m0, m1, m2, m3, out_ref):
    moved = m0[...].astype(F32) + m1[...].astype(F32) + m2[...].astype(F32) + m3[...].astype(F32)
    wide = x_ref[...].astype(F32)
    scale = lax.rsqrt(jnp.mean(wide * wide, axis=-1, keepdims=True) + norm_eps)
    weighted = gain_ref[...] * moved
    moment = jnp.mean(wide * weighted, axis=-1, keepdims=True)
    result = block_ref[...].astype(F32) + scale * weighted - wide * (scale * scale * scale) * moment
    out_ref[...] = result.astype(BF)


def run_finish(kernel, name, out_shape, *operands):
    return pl.pallas_call(
        kernel,
        out_shape=out_shape,
        in_specs=[VMEM_SPEC] * len(operands),
        out_specs=jax.tree.map(lambda leaf: VMEM_SPEC, out_shape),
        compiler_params=pltpu.CompilerParams(vmem_limit_bytes=8 * 2**20),
        name=name,
    )(*operands)


def unset(*leaves):
    return pl.pallas_call(
        lambda *refs: None,
        out_shape=tuple(jax.ShapeDtypeStruct(shape, kind) for shape, kind in leaves),
        out_specs=(ANY_SPEC,) * len(leaves),
        name="unset",
    )()


def shards(tokens, tangent, w_up, w_down, w_router, norm_gain, route_ids):
    micro_count, tok_width, width = tokens.shape
    pipe_count = lax.axis_size("pipe")
    section = lax.axis_index("pipe")
    rank = lax.axis_index("expert")
    expert_y = rank // SIDE
    place_z = rank % SIDE
    w_in = w_up[0]
    w_out = w_down[0]
    gain = norm_gain
    router = jnp.pad(w_router[0], ((0, 0), (0, LANES - EXPERTS)))
    ff = w_in.shape[1]
    rows = SIDE * tok_width
    total = SIDE * rows

    ids = route_ids[0].reshape(micro_count, SIDE, SIDE, tok_width, 2)
    ids = ids.transpose(0, 2, 1, 3, 4).reshape(micro_count, SIDE, rows, 2)
    relative = (place_z - jnp.arange(SIDE)) % SIDE
    ids = jnp.take(ids, relative, axis=1).reshape(micro_count, total, 2)
    lane = jnp.arange(LANES, dtype=jnp.int32)
    contrast = (ids[:, :, 0:1] == lane).astype(F32) - (ids[:, :, 1:2] == lane).astype(F32)
    contrast, router = lax.optimization_barrier((contrast, router))

    start = jnp.stack([tokens, tangent], axis=1)
    groups = [[SIDE * y + z for y in range(SIDE)] for z in range(SIDE)]
    start = lax.all_gather(start, "expert", axis=2, tiled=True, axis_index_groups=groups)

    def reduce_all(parts):
        got = [z_send(parts[4 - d], d) for d in (2, 1, 3)]
        mine = parts[0].astype(F32) + got[0].astype(F32) + got[1].astype(F32) + got[2].astype(F32)
        mine = mine.astype(BF)
        return [mine] + [y_send(mine, d) for d in (2, 1, 3)]

    def make_idx(micro_idx):
        return jnp.stack([micro_idx, expert_y]).astype(jnp.int32)

    def plan(step):
        micro_idx = step // 2
        active = (step >= 0) & (step % 2 == 0) & (micro_idx < micro_count)
        return active, jnp.clip(micro_idx, 0, micro_count - 1)

    def forward_plan(tick):
        return plan(tick - section)

    def backward_plan(tick):
        return plan(tick - (2 * pipe_count - 1 - section))

    def fresh(tick):
        micro_idx = jnp.clip((tick + 1) // 2, 0, micro_count - 1)
        return lax.dynamic_index_in_dim(start, micro_idx, 0, keepdims=False)

    def forward_half(tick, blocks, back, stores, first):
        active, micro_idx = forward_plan(tick)
        last = section == pipe_count - 1

        def run(blocks, back, stores):
            parts, stores = run_forward(
                make_idx(micro_idx), blocks, contrast, gain, router, w_in, w_out, stores
            )
            shape = jax.ShapeDtypeStruct(blocks[0].shape, BF)
            out, final = run_finish(
                forward_finish, "forward_finish",
                (shape, jax.ShapeDtypeStruct(shape.shape[1:], BF)), blocks[0], *reduce_all(parts)
            )
            return out, final, stores

        def rest(blocks, back, stores):
            out = jnp.where(last, fresh(tick), blocks[0]) if first else blocks[0]
            return out, back, stores

        return lax.cond(active, run, rest, blocks, back, stores)

    def store_probe(tick, result, probe_store):
        active, micro_idx = backward_plan(tick)
        write_idx = jnp.where(active, micro_idx, micro_count)
        return lax.dynamic_update_index_in_dim(probe_store, result, write_idx, 0)

    def backward_half(tick, blocks, stores):
        active, micro_idx = backward_plan(tick)

        def run(blocks, stores):
            *parts, inputs = run_backward(
                make_idx(micro_idx), blocks, contrast, router, w_in, w_out, stores
            )
            return run_finish(
                backward_finish, "backward_finish", jax.ShapeDtypeStruct(inputs.shape, BF),
                blocks[0], inputs, gain, *reduce_all(parts)
            )

        return lax.cond(active, run, lambda blocks, stores: blocks[0], blocks, stores)

    *stores, probe_store = unset(
        ((10 * micro_count, rows, width), BF),
        ((2 * micro_count, total, ff), F32),
        ((4 * micro_count, total, ff), BF),
        ((12 * micro_count, 3, total, LANES), F32),
        ((10 * micro_count, rows, width), BF),
    )
    stores = tuple(stores)
    back = jnp.zeros((rows, width), BF)

    def forward_ticks(pair_idx, state):
        out, back, stores = state
        for parity in range(2):
            tick = 2 * pair_idx + parity
            blocks = pipe_gather(out, FIRST_HOPS[parity])
            out, back, stores = forward_half(tick, blocks, back, stores, True)
        return out, back, stores

    def both_ticks(pair_idx, state):
        out, back, stores, probe_store = state
        for parity in range(2):
            tick = 2 * pair_idx + parity
            back_blocks = pipe_gather(back, BACKWARD_HOPS[parity])
            blocks = pipe_gather(out, FORWARD_HOPS[parity])
            probe_store = store_probe(tick - 1, back, probe_store)
            back = backward_half(tick, back_blocks, stores)
            out, back, stores = forward_half(tick, blocks, back, stores, False)
        return out, back, stores, probe_store

    def backward_ticks(pair_idx, state):
        back, probe_store = state
        for parity in range(2):
            tick = 2 * pair_idx + parity
            back_blocks = pipe_gather(back, BACKWARD_HOPS[parity])
            probe_store = store_probe(tick - 1, back, probe_store)
            back = backward_half(tick, back_blocks, stores)
        return back, probe_store

    lead = pipe_count // 2
    turn = lead + micro_count - 1
    out, back, stores = lax.fori_loop(0, lead, forward_ticks, (start[0], back, stores))
    out, back, stores, probe_store = lax.fori_loop(
        lead, turn, both_ticks, (out, back, stores, probe_store)
    )
    back, probe_store = lax.fori_loop(
        turn, pipe_count + micro_count - 1, backward_ticks, (back, probe_store)
    )
    probe_store = store_probe(2 * pipe_count + 2 * micro_count - 3, back, probe_store)
    probes = probe_store[:micro_count].reshape(micro_count, SIDE, tok_width, width)
    probes = lax.dynamic_index_in_dim(probes, expert_y, 1, keepdims=False)
    return probes[None]


def solution(mesh):
    in_specs = (
        P(None, "expert", None),
        P(None, "expert", None),
        P("pipe", None, "expert"),
        P("pipe", "expert", None),
        P("pipe", None, None),
        P("pipe", None),
        P("pipe", None, None, None),
    )
    out_specs = P("pipe", None, "expert", None)
    return jax.shard_map(shards, mesh=mesh, in_specs=in_specs, out_specs=out_specs, check_vma=False)
```

```python
import jax
import jax.numpy as jnp
from jax import lax
from jax.experimental import pallas as pl
from jax.experimental.pallas import tpu as pltpu
from jax.sharding import PartitionSpec as P

EXPERTS = 4
SIDE = 4
LANES = 128
TILE = 512
CHUNK = 512
KERNEL_VMEM = 36 * 2**20

norm_eps = 1e-05
BF = jnp.bfloat16
F32 = jnp.float32


def z_send(block, distance):
    route = [(4 * y + z, 4 * y + (z + distance) % 4) for y in range(4) for z in range(4)]
    return lax.ppermute(block, "expert", route)


def y_send(block, distance):
    route = [(4 * y + z, 4 * ((y + distance) % 4) + z) for y in range(4) for z in range(4)]
    return lax.ppermute(block, "expert", route)


def pipe_send(block, hops, distance):
    route = [
        (16 * p + 4 * y + z, 16 * q + 4 * y + (z + distance) % 4)
        for p, q in hops
        for y in range(4)
        for z in range(4)
    ]
    return lax.ppermute(block, ("pipe", "expert"), route)


def pipe_gather(block, hops):
    sent = {d: pipe_send(block, hops, d) for d in (2, 1, 3, 0)}
    return [sent[d] for d in range(SIDE)]


FORWARD_HOPS = (((1, 2), (3, 4), (5, 6)), ((0, 1), (2, 3), (4, 5), (6, 7)))
FIRST_HOPS = (((7, 0), (1, 2), (3, 4), (5, 6)), FORWARD_HOPS[1])
BACKWARD_HOPS = (((6, 5), (4, 3), (2, 1)), ((7, 6), (5, 4), (3, 2), (1, 0)))


def forward_kernel(idx_ref, a0, a1, a2, a3, c_ref, gain_ref, router_ref, up_hbm, down_hbm,
                   x_in, der_in, hid_in, gate_in, o0, o1, o2, o3, x_store, der_store, hid_store,
                   gate_store, nrm, hid, der, gates, up_ref, down_ref, sems, up_sems, down_sems):
    rows = a0.shape[1]
    total = SIDE * rows
    width, ff = up_ref.shape
    micro_idx = idx_ref[0]

    def up_copy(j):
        span = pl.ds(pl.multiple_of(j * CHUNK, CHUNK), CHUNK)
        return pltpu.make_async_copy(up_hbm.at[:, span], up_ref.at[:, span], up_sems.at[j])

    def down_copy(j):
        span = pl.ds(pl.multiple_of(j * CHUNK, CHUNK), CHUNK)
        return pltpu.make_async_copy(down_hbm.at[:, span], down_ref.at[:, span], down_sems.at[j])

    @pl.loop(0, ff // CHUNK)
    def _(j):
        up_copy(j).start()

    @pl.loop(0, width // CHUNK)
    def _(j):
        down_copy(j).start()

    saves = [
        pltpu.make_async_copy(a0.at[0], x_store.at[micro_idx], sems.at[0]),
        pltpu.make_async_copy(der, der_store.at[micro_idx], sems.at[1]),
        pltpu.make_async_copy(hid.at[pl.ds(0, total)], hid_store.at[micro_idx], sems.at[2]),
        pltpu.make_async_copy(gates, gate_store.at[micro_idx], sems.at[3]),
    ]

    saves[0].start()
    gain = gain_ref[...]
    for d, a in enumerate((a0, a1, a2, a3)):
        x = a[0].astype(F32)
        t = a[1].astype(F32)
        scale = lax.rsqrt(jnp.mean(x * x, axis=-1, keepdims=True) + norm_eps)
        moment = jnp.mean(x * t, axis=-1, keepdims=True)
        nrm[pl.ds(d * rows, rows), :] = (x * scale * gain).astype(BF)
        nrm[pl.ds(total + d * rows, rows), :] = (
            gain * (t * scale - x * (scale * scale * scale) * moment)
        ).astype(BF)
    logits = jnp.dot(nrm[...], router_ref[...], preferred_element_type=F32)
    contrast = c_ref[micro_idx]
    lane = lax.broadcasted_iota(jnp.int32, contrast.shape, 1)
    side = jnp.sum(jnp.where(lane == idx_ref[1], contrast, 0.0), axis=1, keepdims=True)
    margin = jnp.sum(logits[:total] * contrast, axis=1, keepdims=True)
    move = jnp.sum(logits[total:] * contrast, axis=1, keepdims=True)
    first = jax.nn.sigmoid(margin)
    slope = first * (1.0 - first)
    gate = jnp.where(side > 0.5, first, jnp.where(side < -0.5, 1.0 - first, 0.0))
    gates[0] = jnp.broadcast_to(gate, contrast.shape)
    gates[1] = jnp.broadcast_to(side * slope, contrast.shape)
    gates[2] = jnp.broadcast_to(side * slope * move, contrast.shape)
    saves[3].start()

    @pl.loop(0, ff // CHUNK)
    def _(chunk):
        up_copy(chunk).wait()

        @pl.loop(0, CHUNK // TILE)
        def _(tile):
            span = pl.ds(pl.multiple_of(chunk * CHUNK + tile * TILE, TILE), TILE)
            pre_all = jnp.dot(nrm[...], up_ref[:, span], preferred_element_type=F32)
            pre = pre_all[:total]
            logistic = jax.nn.sigmoid(pre)
            derivative = logistic * (1.0 + pre * (1.0 - logistic))
            der[:, span] = derivative
            hid[pl.ds(0, total), span] = (pre * logistic).astype(BF)
            hid[pl.ds(total, total), span] = (derivative * pre_all[total:]).astype(BF)

    saves[1].start()
    saves[2].start()
    gate = gates[0, :, 0:1]
    shift = gates[2, :, 0:1]

    @pl.loop(0, width // CHUNK)
    def _(chunk):
        down_copy(chunk).wait()

        @pl.loop(0, CHUNK // TILE)
        def _(tile):
            span = pl.ds(pl.multiple_of(chunk * CHUNK + tile * TILE, TILE), TILE)
            both = jnp.dot(hid[...], down_ref[:, span], preferred_element_type=F32)
            main = (gate * both[:total]).astype(BF)
            moved = (shift * both[:total] + gate * both[total:]).astype(BF)
            for d, o in enumerate((o0, o1, o2, o3)):
                o[0, :, span] = main[d * rows:(d + 1) * rows]
                o[1, :, span] = moved[d * rows:(d + 1) * rows]

    for save in saves:
        save.wait()


def backward_kernel(idx_ref, b0, b1, b2, b3, c_ref, router_ref, up_hbm, down_hbm, x_store,
                    der_store, hid_store, gate_store, o0, o1, o2, o3, x_ref, cot, back_hid, hid,
                    der, gates, up_ref, down_ref, sems, up_sems, down_sems):
    rows = b0.shape[0]
    total = SIDE * rows
    width, ff = up_ref.shape
    micro_idx = idx_ref[0]

    def up_copy(j):
        span = pl.ds(pl.multiple_of(j * CHUNK, CHUNK), CHUNK)
        return pltpu.make_async_copy(up_hbm.at[span, :], up_ref.at[span, :], up_sems.at[j])

    def down_copy(j):
        span = pl.ds(pl.multiple_of(j * CHUNK, CHUNK), CHUNK)
        return pltpu.make_async_copy(down_hbm.at[span, :], down_ref.at[span, :], down_sems.at[j])

    loads = [
        pltpu.make_async_copy(der_store.at[micro_idx], der, sems.at[0]),
        pltpu.make_async_copy(hid_store.at[micro_idx], hid, sems.at[1]),
        pltpu.make_async_copy(gate_store.at[micro_idx], gates, sems.at[2]),
        pltpu.make_async_copy(x_store.at[micro_idx], x_ref, sems.at[3]),
    ]

    for load in loads:
        load.start()

    @pl.loop(0, ff // CHUNK)
    def _(j):
        down_copy(j).start()

    @pl.loop(0, width // CHUNK)
    def _(j):
        up_copy(j).start()

    @pl.loop(0, width // CHUNK)
    def _(j):
        span = pl.ds(pl.multiple_of(j * CHUNK, CHUNK), CHUNK)
        part = jnp.concatenate([b[:, span] for b in (b0, b1, b2, b3)] * 2, axis=0)
        cot[span, :] = part.T
    for load in loads:
        load.wait()

    def hidden_step(chunk, pull):
        down_copy(chunk).wait()

        def tile_step(tile, pull):
            span = pl.ds(pl.multiple_of(chunk * CHUNK + tile * TILE, TILE), TILE)
            back = jnp.dot(down_ref[span, :], cot[...], preferred_element_type=F32)
            value = hid[:, span].astype(F32)
            both = jnp.concatenate([der[:, span], value], axis=0).T * back
            back_hid[span, :] = both.astype(BF)
            return pull + jnp.sum(both, axis=0, keepdims=True)

        return lax.fori_loop(0, CHUNK // TILE, tile_step, pull)

    pull = lax.fori_loop(0, ff // CHUNK, hidden_step, jnp.zeros((1, 2 * total), F32))
    pull = jnp.broadcast_to(pull, (LANES, 2 * total)).T[total:, 0:1]
    gate = gates[0, :, 0:1]
    grad = gates[1, :, 0:1] * pull
    contrast = c_ref[micro_idx].astype(BF)

    @pl.loop(0, width // CHUNK)
    def _(chunk):
        up_copy(chunk).wait()

        @pl.loop(0, CHUNK // TILE)
        def _(tile):
            span = pl.ds(pl.multiple_of(chunk * CHUNK + tile * TILE, TILE), TILE)
            back = jnp.dot(up_ref[span, :], back_hid[...], preferred_element_type=F32).T[:total]
            gap = lax.dot_general(
                contrast, router_ref[span, :], (((1,), (1,)), ((), ())), preferred_element_type=F32
            )
            part = (gate * back + grad * gap).astype(BF)
            for d, o in enumerate((o0, o1, o2, o3)):
                o[:, span] = part[d * rows:(d + 1) * rows]


SMEM_SPEC = pl.BlockSpec(memory_space=pltpu.SMEM)
VMEM_SPEC = pl.BlockSpec(memory_space=pltpu.VMEM)
ANY_SPEC = pl.BlockSpec(memory_space=pl.ANY)


def run_forward(idx, blocks, contrast, gain, router, w_in, w_out, stores):
    _, rows, width = blocks[0].shape
    ff = w_in.shape[1]
    total = SIDE * rows
    block = jax.ShapeDtypeStruct((2, rows, width), BF)
    out = pl.pallas_call(
        forward_kernel,
        out_shape=(block,) * 4 + tuple(jax.ShapeDtypeStruct(s.shape, s.dtype) for s in stores),
        in_specs=[SMEM_SPEC] + [VMEM_SPEC] * 7 + [ANY_SPEC] * 6,
        out_specs=[VMEM_SPEC] * 4 + [ANY_SPEC] * 4,
        scratch_shapes=[
            pltpu.VMEM((2 * total, width), BF),
            pltpu.VMEM((2 * total, ff), BF),
            pltpu.VMEM((total, ff), F32),
            pltpu.VMEM((3, total, LANES), F32),
            pltpu.VMEM(w_in.shape, BF),
            pltpu.VMEM(w_out.shape, BF),
            pltpu.SemaphoreType.DMA((4,)),
            pltpu.SemaphoreType.DMA((ff // CHUNK,)),
            pltpu.SemaphoreType.DMA((width // CHUNK,)),
        ],
        input_output_aliases={10: 4, 11: 5, 12: 6, 13: 7},
        compiler_params=pltpu.CompilerParams(vmem_limit_bytes=KERNEL_VMEM),
        name="forward_layer",
    )(idx, *blocks, contrast, gain, router, w_in, w_out, *stores)
    return out[:4], tuple(out[4:])


def run_backward(idx, blocks, contrast, router, w_in, w_out, stores):
    rows, width = blocks[0].shape
    ff = w_in.shape[1]
    total = SIDE * rows
    block = jax.ShapeDtypeStruct((rows, width), BF)
    return pl.pallas_call(
        backward_kernel,
        out_shape=(block,) * 5,
        in_specs=[SMEM_SPEC] + [VMEM_SPEC] * 6 + [ANY_SPEC] * 6,
        out_specs=[VMEM_SPEC] * 5,
        scratch_shapes=[
            pltpu.VMEM((width, 2 * total), BF),
            pltpu.VMEM((ff, 2 * total), BF),
            pltpu.VMEM((total, ff), BF),
            pltpu.VMEM((total, ff), F32),
            pltpu.VMEM((3, total, LANES), F32),
            pltpu.VMEM(w_in.shape, BF),
            pltpu.VMEM(w_out.shape, BF),
            pltpu.SemaphoreType.DMA((4,)),
            pltpu.SemaphoreType.DMA((width // CHUNK,)),
            pltpu.SemaphoreType.DMA((ff // CHUNK,)),
        ],
        compiler_params=pltpu.CompilerParams(vmem_limit_bytes=KERNEL_VMEM),
        name="backward_layer",
    )(idx, *blocks, contrast, router, w_in, w_out, *stores)


def forward_finish(block_ref, m0, m1, m2, m3, out_ref):
    moved = m0[...].astype(F32) + m1[...].astype(F32) + m2[...].astype(F32) + m3[...].astype(F32)
    out_ref[...] = (block_ref[...].astype(F32) + moved).astype(BF)


def tangent_finish(block_ref, m0, m1, m2, m3, out_ref):
    moved = m0[...].astype(F32) + m1[...].astype(F32) + m2[...].astype(F32) + m3[...].astype(F32)
    out_ref[...] = (block_ref[1].astype(F32) + moved).astype(BF)


def backward_finish(block_ref, x_ref, gain_ref, m0, m1, m2, m3, out_ref):
    moved = m0[...].astype(F32) + m1[...].astype(F32) + m2[...].astype(F32) + m3[...].astype(F32)
    wide = x_ref[...].astype(F32)
    scale = lax.rsqrt(jnp.mean(wide * wide, axis=-1, keepdims=True) + norm_eps)
    weighted = gain_ref[...] * moved
    moment = jnp.mean(wide * weighted, axis=-1, keepdims=True)
    result = block_ref[...].astype(F32) + scale * weighted - wide * (scale * scale * scale) * moment
    out_ref[...] = result.astype(BF)


def run_finish(kernel, name, out_shape, *operands):
    return pl.pallas_call(
        kernel,
        out_shape=out_shape,
        in_specs=[VMEM_SPEC] * len(operands),
        out_specs=jax.tree.map(lambda leaf: VMEM_SPEC, out_shape),
        compiler_params=pltpu.CompilerParams(vmem_limit_bytes=8 * 2**20),
        name=name,
    )(*operands)


def unset(*leaves):
    return pl.pallas_call(
        lambda *refs: None,
        out_shape=tuple(jax.ShapeDtypeStruct(shape, kind) for shape, kind in leaves),
        out_specs=(ANY_SPEC,) * len(leaves),
        name="unset",
    )()


def shards(tokens, tangent, w_up, w_down, w_router, norm_gain, route_ids):
    micro_count, tok_width, width = tokens.shape
    pipe_count = lax.axis_size("pipe")
    section = lax.axis_index("pipe")
    rank = lax.axis_index("expert")
    expert_y = rank // SIDE
    place_z = rank % SIDE
    w_in = w_up[0]
    w_out = w_down[0]
    gain = norm_gain
    router = jnp.pad(w_router[0], ((0, 0), (0, LANES - EXPERTS)))
    ff = w_in.shape[1]
    rows = SIDE * tok_width
    total = SIDE * rows

    ids = route_ids[0].reshape(micro_count, SIDE, SIDE, tok_width, 2)
    ids = ids.transpose(0, 2, 1, 3, 4).reshape(micro_count, SIDE, rows, 2)
    relative = (place_z - jnp.arange(SIDE)) % SIDE
    ids = jnp.take(ids, relative, axis=1).reshape(micro_count, total, 2)
    lane = jnp.arange(LANES, dtype=jnp.int32)
    contrast = (ids[:, :, 0:1] == lane).astype(F32) - (ids[:, :, 1:2] == lane).astype(F32)
    contrast, router = lax.optimization_barrier((contrast, router))

    start = jnp.stack([tokens, tangent], axis=1)
    groups = [[SIDE * y + z for y in range(SIDE)] for z in range(SIDE)]
    start = lax.all_gather(start, "expert", axis=2, tiled=True, axis_index_groups=groups)

    def reduce_all(parts):
        got = [z_send(parts[4 - d], d) for d in (2, 1, 3)]
        mine = parts[0].astype(F32) + got[0].astype(F32) + got[1].astype(F32) + got[2].astype(F32)
        mine = mine.astype(BF)
        return [mine] + [y_send(mine, d) for d in (2, 1, 3)]

    def make_idx(micro_idx):
        return jnp.stack([micro_idx, expert_y]).astype(jnp.int32)

    def plan(step):
        micro_idx = step // 2
        active = (step >= 0) & (step % 2 == 0) & (micro_idx < micro_count)
        return active, jnp.clip(micro_idx, 0, micro_count - 1)

    def forward_plan(tick):
        return plan(tick - section)

    def backward_plan(tick):
        return plan(tick - (2 * pipe_count - 1 - section))

    def fresh(tick):
        micro_idx = jnp.clip((tick + 1) // 2, 0, micro_count - 1)
        return lax.dynamic_index_in_dim(start, micro_idx, 0, keepdims=False)

    def forward_half(tick, parity, blocks, kept, stores, first):
        active, micro_idx = forward_plan(tick)
        last = section == pipe_count - 1
        block = jax.ShapeDtypeStruct(blocks[0].shape, BF)
        row_block = jax.ShapeDtypeStruct(block.shape[1:], BF)

        def pass_on(blocks, kept, parts):
            out = run_finish(
                forward_finish, "forward_finish", block, blocks[0], *reduce_all(parts)
            )
            return out, kept

        def turn_round(blocks, kept, parts):
            final = run_finish(
                tangent_finish, "tangent_finish", row_block, blocks[0],
                *reduce_all([part[1] for part in parts])
            )
            sent = {d: z_send(final, d) for d in (2, 1, 3)}
            return blocks[0], [final] + [sent[d] for d in (1, 2, 3)]

        def run(blocks, kept, stores):
            parts, stores = run_forward(
                make_idx(micro_idx), blocks, contrast, gain, router, w_in, w_out, stores
            )
            if parity == 0:
                return *pass_on(blocks, kept, parts), stores
            return *lax.cond(last, turn_round, pass_on, blocks, kept, parts), stores

        def rest(blocks, kept, stores):
            out = jnp.where(last, fresh(tick), blocks[0]) if first else blocks[0]
            return out, kept, stores

        return lax.cond(active, run, rest, blocks, kept, stores)

    def store_probe(tick, result, probe_store):
        active, micro_idx = backward_plan(tick)
        write_idx = jnp.where(active, micro_idx, micro_count)
        return lax.dynamic_update_index_in_dim(probe_store, result, write_idx, 0)

    def backward_half(tick, parity, blocks, kept, stores):
        active, micro_idx = backward_plan(tick)
        last = section == pipe_count - 1

        def run(blocks, kept, stores):
            if parity == 0:
                blocks = [jnp.where(last, k, b) for k, b in zip(kept, blocks)]
            *parts, inputs = run_backward(
                make_idx(micro_idx), blocks, contrast, router, w_in, w_out, stores
            )
            return run_finish(
                backward_finish, "backward_finish", jax.ShapeDtypeStruct(inputs.shape, BF),
                blocks[0], inputs, gain, *reduce_all(parts)
            )

        def rest(blocks, kept, stores):
            return blocks[0]

        return lax.cond(active, run, rest, blocks, kept, stores)

    *stores, probe_store = unset(
        ((10 * micro_count, rows, width), BF),
        ((2 * micro_count, total, ff), F32),
        ((4 * micro_count, total, ff), BF),
        ((12 * micro_count, 3, total, LANES), F32),
        ((10 * micro_count, rows, width), BF),
    )
    stores = tuple(stores)
    back = jnp.zeros((rows, width), BF)
    kept = [back] * SIDE

    def forward_ticks(pair_idx, state):
        out, kept, stores = state
        for parity in range(2):
            tick = 2 * pair_idx + parity
            blocks = pipe_gather(out, FIRST_HOPS[parity])
            out, kept, stores = forward_half(tick, parity, blocks, kept, stores, True)
        return out, kept, stores

    def both_ticks(pair_idx, state):
        out, back, kept, stores, probe_store = state
        for parity in range(2):
            tick = 2 * pair_idx + parity
            back_blocks = pipe_gather(back, BACKWARD_HOPS[parity])
            blocks = pipe_gather(out, FORWARD_HOPS[parity])
            probe_store = store_probe(tick - 1, back, probe_store)
            back = backward_half(tick, parity, back_blocks, kept, stores)
            out, kept, stores = forward_half(tick, parity, blocks, kept, stores, False)
        return out, back, kept, stores, probe_store

    def backward_ticks(pair_idx, state):
        back, probe_store = state
        for parity in range(2):
            tick = 2 * pair_idx + parity
            back_blocks = pipe_gather(back, BACKWARD_HOPS[parity])
            probe_store = store_probe(tick - 1, back, probe_store)
            back = backward_half(tick, parity, back_blocks, kept, stores)
        return back, probe_store

    lead = pipe_count // 2
    turn = lead + micro_count - 1
    out, kept, stores = lax.fori_loop(0, lead, forward_ticks, (start[0], kept, stores))
    out, back, kept, stores, probe_store = lax.fori_loop(
        lead, turn, both_ticks, (out, back, kept, stores, probe_store)
    )
    back, probe_store = lax.fori_loop(
        turn, pipe_count + micro_count - 1, backward_ticks, (back, probe_store)
    )
    probe_store = store_probe(2 * pipe_count + 2 * micro_count - 3, back, probe_store)
    probes = probe_store[:micro_count].reshape(micro_count, SIDE, tok_width, width)
    probes = lax.dynamic_index_in_dim(probes, expert_y, 1, keepdims=False)
    return probes[None]


def solution(mesh):
    in_specs = (
        P(None, "expert", None),
        P(None, "expert", None),
        P("pipe", None, "expert"),
        P("pipe", "expert", None),
        P("pipe", None, None),
        P("pipe", None),
        P("pipe", None, None, None),
    )
    out_specs = P("pipe", None, "expert", None)
    return jax.shard_map(shards, mesh=mesh, in_specs=in_specs, out_specs=out_specs, check_vma=False)
```

```python
import jax
import jax.numpy as jnp
from jax import lax
from jax.experimental import pallas as pl
from jax.experimental.pallas import tpu as pltpu
from jax.sharding import PartitionSpec as P

EXPERTS = 4
SIDE = 4
LANES = 128
TILE = 512
CHUNK = 512
KERNEL_VMEM = 36 * 2**20

norm_eps = 1e-05
BF = jnp.bfloat16
F32 = jnp.float32


def z_send(block, distance):
    route = [(4 * y + z, 4 * y + (z + distance) % 4) for y in range(4) for z in range(4)]
    return lax.ppermute(block, "expert", route)


def y_send(block, distance):
    route = [(4 * y + z, 4 * ((y + distance) % 4) + z) for y in range(4) for z in range(4)]
    return lax.ppermute(block, "expert", route)


def pipe_send(block, hops, distance):
    route = [
        (16 * p + 4 * y + z, 16 * q + 4 * y + (z + distance) % 4)
        for p, q in hops
        for y in range(4)
        for z in range(4)
    ]
    return lax.ppermute(block, ("pipe", "expert"), route)


def pipe_gather(block, hops):
    sent = {d: pipe_send(block, hops, d) for d in (2, 1, 3, 0)}
    return [sent[d] for d in range(SIDE)]


FORWARD_HOPS = (((7, 0), (1, 2), (3, 4), (5, 6)), ((0, 1), (2, 3), (4, 5), (6, 7)))
BACKWARD_HOPS = (((7, 7), (6, 5), (4, 3), (2, 1)), ((7, 6), (5, 4), (3, 2), (1, 0)))
SWAP_HOPS = (
    ((7, 7), (1, 2), (3, 4), (5, 6), (2, 1), (4, 3), (6, 5)),
    FORWARD_HOPS[1] + BACKWARD_HOPS[1],
)


def forward_kernel(idx_ref, a0, a1, a2, a3, c_ref, gain_ref, router_ref, up_hbm, down_hbm,
                   x_in, der_in, hid_in, gate_in, o0, o1, o2, o3, x_store, der_store, hid_store,
                   gate_store, nrm, hid, der, gates, up_ref, down_ref, sems, up_sems, down_sems):
    rows = a0.shape[1]
    total = SIDE * rows
    width, ff = up_ref.shape
    micro_idx = idx_ref[0]

    def up_copy(j):
        span = pl.ds(pl.multiple_of(j * CHUNK, CHUNK), CHUNK)
        return pltpu.make_async_copy(up_hbm.at[:, span], up_ref.at[:, span], up_sems.at[j])

    def down_copy(j):
        span = pl.ds(pl.multiple_of(j * CHUNK, CHUNK), CHUNK)
        return pltpu.make_async_copy(down_hbm.at[:, span], down_ref.at[:, span], down_sems.at[j])

    @pl.loop(0, ff // CHUNK)
    def _(j):
        up_copy(j).start()

    @pl.loop(0, width // CHUNK)
    def _(j):
        down_copy(j).start()

    saves = [
        pltpu.make_async_copy(a0.at[0], x_store.at[micro_idx], sems.at[0]),
        pltpu.make_async_copy(der, der_store.at[micro_idx], sems.at[1]),
        pltpu.make_async_copy(hid.at[pl.ds(0, total)], hid_store.at[micro_idx], sems.at[2]),
        pltpu.make_async_copy(gates, gate_store.at[micro_idx], sems.at[3]),
    ]

    saves[0].start()
    gain = gain_ref[...]
    for d, a in enumerate((a0, a1, a2, a3)):
        x = a[0].astype(F32)
        t = a[1].astype(F32)
        scale = lax.rsqrt(jnp.mean(x * x, axis=-1, keepdims=True) + norm_eps)
        moment = jnp.mean(x * t, axis=-1, keepdims=True)
        nrm[pl.ds(d * rows, rows), :] = (x * scale * gain).astype(BF)
        nrm[pl.ds(total + d * rows, rows), :] = (
            gain * (t * scale - x * (scale * scale * scale) * moment)
        ).astype(BF)
    logits = jnp.dot(nrm[...], router_ref[...], preferred_element_type=F32)
    contrast = c_ref[micro_idx]
    lane = lax.broadcasted_iota(jnp.int32, contrast.shape, 1)
    side = jnp.sum(jnp.where(lane == idx_ref[1], contrast, 0.0), axis=1, keepdims=True)
    margin = jnp.sum(logits[:total] * contrast, axis=1, keepdims=True)
    move = jnp.sum(logits[total:] * contrast, axis=1, keepdims=True)
    first = jax.nn.sigmoid(margin)
    slope = first * (1.0 - first)
    gate = jnp.where(side > 0.5, first, jnp.where(side < -0.5, 1.0 - first, 0.0))
    gates[0] = jnp.broadcast_to(gate, contrast.shape)
    gates[1] = jnp.broadcast_to(side * slope, contrast.shape)
    gates[2] = jnp.broadcast_to(side * slope * move, contrast.shape)
    saves[3].start()

    @pl.loop(0, ff // CHUNK)
    def _(chunk):
        up_copy(chunk).wait()

        @pl.loop(0, CHUNK // TILE)
        def _(tile):
            span = pl.ds(pl.multiple_of(chunk * CHUNK + tile * TILE, TILE), TILE)
            pre_all = jnp.dot(nrm[...], up_ref[:, span], preferred_element_type=F32)
            pre = pre_all[:total]
            logistic = jax.nn.sigmoid(pre)
            derivative = logistic * (1.0 + pre * (1.0 - logistic))
            der[:, span] = derivative
            hid[pl.ds(0, total), span] = (pre * logistic).astype(BF)
            hid[pl.ds(total, total), span] = (derivative * pre_all[total:]).astype(BF)

    saves[1].start()
    saves[2].start()
    gate = gates[0, :, 0:1]
    shift = gates[2, :, 0:1]

    @pl.loop(0, width // CHUNK)
    def _(chunk):
        down_copy(chunk).wait()

        @pl.loop(0, CHUNK // TILE)
        def _(tile):
            span = pl.ds(pl.multiple_of(chunk * CHUNK + tile * TILE, TILE), TILE)
            both = jnp.dot(hid[...], down_ref[:, span], preferred_element_type=F32)
            main = (gate * both[:total]).astype(BF)
            moved = (shift * both[:total] + gate * both[total:]).astype(BF)
            for d, o in enumerate((o0, o1, o2, o3)):
                o[0, :, span] = main[d * rows:(d + 1) * rows]
                o[1, :, span] = moved[d * rows:(d + 1) * rows]

    for save in saves:
        save.wait()


def backward_kernel(idx_ref, b0, b1, b2, b3, c_ref, router_ref, up_hbm, down_hbm, x_store,
                    der_store, hid_store, gate_store, o0, o1, o2, o3, x_ref, cot, back_hid, hid,
                    der, gates, up_ref, down_ref, sems, up_sems, down_sems):
    rows = b0.shape[1]
    total = SIDE * rows
    width, ff = up_ref.shape
    micro_idx = idx_ref[0]
    slot = idx_ref[2]

    def up_copy(j):
        span = pl.ds(pl.multiple_of(j * CHUNK, CHUNK), CHUNK)
        return pltpu.make_async_copy(up_hbm.at[span, :], up_ref.at[span, :], up_sems.at[j])

    def down_copy(j):
        span = pl.ds(pl.multiple_of(j * CHUNK, CHUNK), CHUNK)
        return pltpu.make_async_copy(down_hbm.at[span, :], down_ref.at[span, :], down_sems.at[j])

    loads = [
        pltpu.make_async_copy(der_store.at[micro_idx], der, sems.at[0]),
        pltpu.make_async_copy(hid_store.at[micro_idx], hid, sems.at[1]),
        pltpu.make_async_copy(gate_store.at[micro_idx], gates, sems.at[2]),
        pltpu.make_async_copy(x_store.at[micro_idx], x_ref, sems.at[3]),
    ]

    for load in loads:
        load.start()

    @pl.loop(0, ff // CHUNK)
    def _(j):
        down_copy(j).start()

    @pl.loop(0, width // CHUNK)
    def _(j):
        up_copy(j).start()

    @pl.loop(0, width // CHUNK)
    def _(j):
        span = pl.ds(pl.multiple_of(j * CHUNK, CHUNK), CHUNK)
        part = jnp.concatenate([b[slot, :, span] for b in (b0, b1, b2, b3)] * 2, axis=0)
        cot[span, :] = part.T
    for load in loads:
        load.wait()

    def hidden_step(chunk, pull):
        down_copy(chunk).wait()

        def tile_step(tile, pull):
            span = pl.ds(pl.multiple_of(chunk * CHUNK + tile * TILE, TILE), TILE)
            back = jnp.dot(down_ref[span, :], cot[...], preferred_element_type=F32)
            value = hid[:, span].astype(F32)
            both = jnp.concatenate([der[:, span], value], axis=0).T * back
            back_hid[span, :] = both.astype(BF)
            return pull + jnp.sum(both, axis=0, keepdims=True)

        return lax.fori_loop(0, CHUNK // TILE, tile_step, pull)

    pull = lax.fori_loop(0, ff // CHUNK, hidden_step, jnp.zeros((1, 2 * total), F32))
    pull = jnp.broadcast_to(pull, (LANES, 2 * total)).T[total:, 0:1]
    gate = gates[0, :, 0:1]
    grad = gates[1, :, 0:1] * pull
    contrast = c_ref[micro_idx].astype(BF)

    @pl.loop(0, width // CHUNK)
    def _(chunk):
        up_copy(chunk).wait()

        @pl.loop(0, CHUNK // TILE)
        def _(tile):
            span = pl.ds(pl.multiple_of(chunk * CHUNK + tile * TILE, TILE), TILE)
            back = jnp.dot(up_ref[span, :], back_hid[...], preferred_element_type=F32).T[:total]
            gap = lax.dot_general(
                contrast, router_ref[span, :], (((1,), (1,)), ((), ())), preferred_element_type=F32
            )
            part = (gate * back + grad * gap).astype(BF)
            for d, o in enumerate((o0, o1, o2, o3)):
                o[:, span] = part[d * rows:(d + 1) * rows]


SMEM_SPEC = pl.BlockSpec(memory_space=pltpu.SMEM)
VMEM_SPEC = pl.BlockSpec(memory_space=pltpu.VMEM)
ANY_SPEC = pl.BlockSpec(memory_space=pl.ANY)


def run_forward(idx, blocks, contrast, gain, router, w_in, w_out, stores):
    _, rows, width = blocks[0].shape
    ff = w_in.shape[1]
    total = SIDE * rows
    block = jax.ShapeDtypeStruct((2, rows, width), BF)
    out = pl.pallas_call(
        forward_kernel,
        out_shape=(block,) * 4 + tuple(jax.ShapeDtypeStruct(s.shape, s.dtype) for s in stores),
        in_specs=[SMEM_SPEC] + [VMEM_SPEC] * 7 + [ANY_SPEC] * 6,
        out_specs=[VMEM_SPEC] * 4 + [ANY_SPEC] * 4,
        scratch_shapes=[
            pltpu.VMEM((2 * total, width), BF),
            pltpu.VMEM((2 * total, ff), BF),
            pltpu.VMEM((total, ff), F32),
            pltpu.VMEM((3, total, LANES), F32),
            pltpu.VMEM(w_in.shape, BF),
            pltpu.VMEM(w_out.shape, BF),
            pltpu.SemaphoreType.DMA((4,)),
            pltpu.SemaphoreType.DMA((ff // CHUNK,)),
            pltpu.SemaphoreType.DMA((width // CHUNK,)),
        ],
        input_output_aliases={10: 4, 11: 5, 12: 6, 13: 7},
        compiler_params=pltpu.CompilerParams(vmem_limit_bytes=KERNEL_VMEM),
        name="forward_layer",
    )(idx, *blocks, contrast, gain, router, w_in, w_out, *stores)
    return out[:4], tuple(out[4:])


def run_backward(idx, blocks, contrast, router, w_in, w_out, stores):
    _, rows, width = blocks[0].shape
    ff = w_in.shape[1]
    total = SIDE * rows
    block = jax.ShapeDtypeStruct((rows, width), BF)
    return pl.pallas_call(
        backward_kernel,
        out_shape=(block,) * 5,
        in_specs=[SMEM_SPEC] + [VMEM_SPEC] * 6 + [ANY_SPEC] * 6,
        out_specs=[VMEM_SPEC] * 5,
        scratch_shapes=[
            pltpu.VMEM((width, 2 * total), BF),
            pltpu.VMEM((ff, 2 * total), BF),
            pltpu.VMEM((total, ff), BF),
            pltpu.VMEM((total, ff), F32),
            pltpu.VMEM((3, total, LANES), F32),
            pltpu.VMEM(w_in.shape, BF),
            pltpu.VMEM(w_out.shape, BF),
            pltpu.SemaphoreType.DMA((4,)),
            pltpu.SemaphoreType.DMA((width // CHUNK,)),
            pltpu.SemaphoreType.DMA((ff // CHUNK,)),
        ],
        compiler_params=pltpu.CompilerParams(vmem_limit_bytes=KERNEL_VMEM),
        name="backward_layer",
    )(idx, *blocks, contrast, router, w_in, w_out, *stores)


def forward_finish(block_ref, m0, m1, m2, m3, out_ref):
    moved = m0[...].astype(F32) + m1[...].astype(F32) + m2[...].astype(F32) + m3[...].astype(F32)
    out_ref[...] = (block_ref[...].astype(F32) + moved).astype(BF)


def backward_finish(idx_ref, block_ref, x_ref, gain_ref, m0, m1, m2, m3, out_ref):
    moved = m0[...].astype(F32) + m1[...].astype(F32) + m2[...].astype(F32) + m3[...].astype(F32)
    wide = x_ref[...].astype(F32)
    scale = lax.rsqrt(jnp.mean(wide * wide, axis=-1, keepdims=True) + norm_eps)
    weighted = gain_ref[...] * moved
    moment = jnp.mean(wide * weighted, axis=-1, keepdims=True)
    block = block_ref[idx_ref[2]].astype(F32)
    result = block + scale * weighted - wide * (scale * scale * scale) * moment
    for slot in range(out_ref.shape[0]):
        out_ref[slot] = result.astype(BF)


def run_finish(kernel, name, scalars, *operands):
    block = operands[0]
    return pl.pallas_call(
        kernel,
        out_shape=jax.ShapeDtypeStruct(block.shape, block.dtype),
        in_specs=[SMEM_SPEC] * len(scalars) + [VMEM_SPEC] * len(operands),
        out_specs=VMEM_SPEC,
        compiler_params=pltpu.CompilerParams(vmem_limit_bytes=8 * 2**20),
        name=name,
    )(*scalars, *operands)


def unset(*leaves):
    return pl.pallas_call(
        lambda *refs: None,
        out_shape=tuple(jax.ShapeDtypeStruct(shape, kind) for shape, kind in leaves),
        out_specs=(ANY_SPEC,) * len(leaves),
        name="unset",
    )()


def shards(tokens, tangent, w_up, w_down, w_router, norm_gain, route_ids):
    micro_count, tok_width, width = tokens.shape
    pipe_count = lax.axis_size("pipe")
    section = lax.axis_index("pipe")
    rank = lax.axis_index("expert")
    expert_y = rank // SIDE
    place_z = rank % SIDE
    w_in = w_up[0]
    w_out = w_down[0]
    gain = norm_gain
    router = jnp.pad(w_router[0], ((0, 0), (0, LANES - EXPERTS)))
    ff = w_in.shape[1]
    rows = SIDE * tok_width
    total = SIDE * rows

    ids = route_ids[0].reshape(micro_count, SIDE, SIDE, tok_width, 2)
    ids = ids.transpose(0, 2, 1, 3, 4).reshape(micro_count, SIDE, rows, 2)
    relative = (place_z - jnp.arange(SIDE)) % SIDE
    ids = jnp.take(ids, relative, axis=1).reshape(micro_count, total, 2)
    lane = jnp.arange(LANES, dtype=jnp.int32)
    contrast = (ids[:, :, 0:1] == lane).astype(F32) - (ids[:, :, 1:2] == lane).astype(F32)
    contrast, router = lax.optimization_barrier((contrast, router))

    start = jnp.stack([tokens, tangent], axis=1)
    groups = [[SIDE * y + z for y in range(SIDE)] for z in range(SIDE)]
    start = lax.all_gather(start, "expert", axis=2, tiled=True, axis_index_groups=groups)

    def reduce_all(parts):
        got = [z_send(parts[4 - d], d) for d in (2, 1, 3)]
        mine = parts[0].astype(F32) + got[0].astype(F32) + got[1].astype(F32) + got[2].astype(F32)
        mine = mine.astype(BF)
        return [mine] + [y_send(mine, d) for d in (2, 1, 3)]

    def make_idx(micro_idx, slot):
        return jnp.stack([micro_idx, expert_y, slot]).astype(jnp.int32)

    def plan(step):
        micro_idx = step // 2
        active = (step >= 0) & (step % 2 == 0) & (micro_idx < micro_count)
        return active, jnp.clip(micro_idx, 0, micro_count - 1)

    def forward_plan(tick):
        return plan(tick - section)

    def backward_plan(tick):
        return plan(tick - (2 * pipe_count - 1 - section))

    def fresh(tick):
        micro_idx = jnp.clip((tick + 1) // 2, 0, micro_count - 1)
        return lax.dynamic_index_in_dim(start, micro_idx, 0, keepdims=False)

    last = section == pipe_count - 1

    def forward_run(micro_idx, blocks, stores):
        parts, stores = run_forward(
            make_idx(micro_idx, 0), blocks, contrast, gain, router, w_in, w_out, stores
        )
        out = run_finish(forward_finish, "forward_finish", (), blocks[0], *reduce_all(parts))
        return out, stores

    def backward_run(micro_idx, slot, blocks, stores):
        idx = make_idx(micro_idx, slot)
        *parts, inputs = run_backward(idx, blocks, contrast, router, w_in, w_out, stores)
        return run_finish(
            backward_finish, "backward_finish", (idx,), blocks[0], inputs, gain, *reduce_all(parts)
        )

    def forward_half(tick, blocks, stores):
        active, micro_idx = forward_plan(tick)

        def run(blocks, stores):
            return forward_run(micro_idx, blocks, stores)

        def rest(blocks, stores):
            return jnp.where(last, fresh(tick), blocks[0]), stores

        return lax.cond(active, run, rest, blocks, stores)

    def backward_half(tick, blocks, stores):
        active, micro_idx = backward_plan(tick)

        def run(blocks, stores):
            return backward_run(micro_idx, 0, blocks, stores)

        return lax.cond(active, run, lambda blocks, stores: blocks[0], blocks, stores)

    def either_half(tick, blocks, stores):
        forward_active, forward_idx = forward_plan(tick)
        backward_active, backward_idx = backward_plan(tick)

        def rest(blocks, stores):
            return blocks[0], stores

        def forward(blocks, stores):
            return forward_run(forward_idx, blocks, stores)

        def backward(blocks, stores):
            slot = last.astype(jnp.int32)
            return backward_run(backward_idx, slot, blocks, stores), stores

        branch = jnp.where(forward_active, 1, jnp.where(backward_active, 2, 0))
        return lax.switch(branch, (rest, forward, backward), blocks, stores)

    def store_probe(tick, result, probe_store):
        active, micro_idx = backward_plan(tick)
        write_idx = jnp.where(active, micro_idx, micro_count)
        return lax.dynamic_update_index_in_dim(probe_store, result, write_idx, 0)

    *stores, probe_store = unset(
        ((10 * micro_count, rows, width), BF),
        ((2 * micro_count, total, ff), F32),
        ((4 * micro_count, total, ff), BF),
        ((12 * micro_count, 3, total, LANES), F32),
        ((10 * micro_count, rows, width), BF),
    )
    stores = tuple(stores)
    def forward_ticks(pair_idx, state):
        send, stores = state
        for parity in range(2):
            blocks = pipe_gather(send, FORWARD_HOPS[parity])
            send, stores = forward_half(2 * pair_idx + parity, blocks, stores)
        return send, stores

    def both_ticks(pair_idx, state):
        send, stores, probe_store = state
        for parity in range(2):
            tick = 2 * pair_idx + parity
            blocks = pipe_gather(send, SWAP_HOPS[parity])
            probe_store = store_probe(tick - 1, send[0], probe_store)
            send, stores = either_half(tick, blocks, stores)
        return send, stores, probe_store

    def backward_ticks(pair_idx, state):
        back, probe_store = state
        for parity in range(2):
            tick = 2 * pair_idx + parity
            blocks = pipe_gather(back, BACKWARD_HOPS[parity])
            probe_store = store_probe(tick - 1, back[0], probe_store)
            back = backward_half(tick, blocks, stores)
        return back, probe_store

    lead = pipe_count // 2
    turn = lead + micro_count - 1
    send, stores = lax.fori_loop(0, lead, forward_ticks, (start[0], stores))
    send, stores, probe_store = lax.fori_loop(lead, turn, both_ticks, (send, stores, probe_store))
    back = jnp.where(last, send[1], send[0])[None]
    back, probe_store = lax.fori_loop(
        turn, pipe_count + micro_count - 1, backward_ticks, (back, probe_store)
    )
    back = back[0]
    probe_store = store_probe(2 * pipe_count + 2 * micro_count - 3, back, probe_store)
    probes = probe_store[:micro_count].reshape(micro_count, SIDE, tok_width, width)
    probes = lax.dynamic_index_in_dim(probes, expert_y, 1, keepdims=False)
    return probes[None]


def solution(mesh):
    in_specs = (
        P(None, "expert", None),
        P(None, "expert", None),
        P("pipe", None, "expert"),
        P("pipe", "expert", None),
        P("pipe", None, None),
        P("pipe", None),
        P("pipe", None, None, None),
    )
    out_specs = P("pipe", None, "expert", None)
    return jax.shard_map(shards, mesh=mesh, in_specs=in_specs, out_specs=out_specs, check_vma=False)
```

```python
import jax
import jax.numpy as jnp
from jax import lax
from jax.experimental import pallas as pl
from jax.experimental.pallas import tpu as pltpu
from jax.sharding import PartitionSpec as P

EXPERTS = 4
SIDE = 4
LANES = 128
TILE = 512
CHUNK = 512
KERNEL_VMEM = 36 * 2**20
LOADED_VMEM = 24 * 2**20

norm_eps = 1e-05
BF = jnp.bfloat16
F32 = jnp.float32


def z_send(block, distance):
    route = [(4 * y + z, 4 * y + (z + distance) % 4) for y in range(4) for z in range(4)]
    return lax.ppermute(block, "expert", route)


def y_send(block, distance):
    route = [(4 * y + z, 4 * ((y + distance) % 4) + z) for y in range(4) for z in range(4)]
    return lax.ppermute(block, "expert", route)


def pipe_send(block, hops, distance):
    route = [
        (16 * p + 4 * y + z, 16 * q + 4 * y + (z + distance) % 4)
        for p, q in hops
        for y in range(4)
        for z in range(4)
    ]
    return lax.ppermute(block, ("pipe", "expert"), route)


def pipe_gather(block, hops):
    sent = {d: pipe_send(block, hops, d) for d in (2, 1, 3, 0)}
    return [sent[d] for d in range(SIDE)]


FORWARD_HOPS = (((7, 0), (1, 2), (3, 4), (5, 6)), ((0, 1), (2, 3), (4, 5), (6, 7)))
BACKWARD_HOPS = (((7, 7), (6, 5), (4, 3), (2, 1)), ((7, 6), (5, 4), (3, 2), (1, 0)))
SWAP_HOPS = (
    ((7, 7), (1, 2), (3, 4), (5, 6), (2, 1), (4, 3), (6, 5)),
    FORWARD_HOPS[1] + BACKWARD_HOPS[1],
)


def forward_kernel(idx_ref, a0, a1, a2, a3, c_ref, gain_ref, router_ref, up_hbm, down_hbm,
                   x_in, der_in, hid_in, gate_in, o0, o1, o2, o3, x_store, der_store, hid_store,
                   gate_store, nrm, hid, der, gates, sems, up_ref, down_ref, up_sems, down_sems):
    _, ff = up_ref.shape
    width = down_ref.shape[1]

    def up_copy(j):
        span = pl.ds(pl.multiple_of(j * CHUNK, CHUNK), CHUNK)
        return pltpu.make_async_copy(up_hbm.at[:, span], up_ref.at[:, span], up_sems.at[j])

    def down_copy(j):
        span = pl.ds(pl.multiple_of(j * CHUNK, CHUNK), CHUNK)
        return pltpu.make_async_copy(down_hbm.at[:, span], down_ref.at[:, span], down_sems.at[j])

    @pl.loop(0, ff // CHUNK)
    def _(j):
        up_copy(j).start()

    @pl.loop(0, width // CHUNK)
    def _(j):
        down_copy(j).start()

    forward_body(idx_ref, (a0, a1, a2, a3), c_ref, gain_ref, router_ref, up_ref, down_ref,
                 (o0, o1, o2, o3), x_store, der_store, hid_store, gate_store, nrm, hid, der, gates,
                 sems, lambda j: up_copy(j).wait(), lambda j: down_copy(j).wait())


def loaded_kernel(idx_ref, a0, a1, a2, a3, c_ref, gain_ref, router_ref, up_ref, down_ref,
                  x_in, der_in, hid_in, gate_in, o0, o1, o2, o3, x_store, der_store, hid_store,
                  gate_store, nrm, hid, der, gates, sems):
    @pl.when(idx_ref[2] == 1)
    def _():
        forward_body(idx_ref, (a0, a1, a2, a3), c_ref, gain_ref, router_ref, up_ref, down_ref,
                     (o0, o1, o2, o3), x_store, der_store, hid_store, gate_store, nrm, hid, der,
                     gates, sems, lambda j: None, lambda j: None)


def forward_body(idx_ref, blocks, c_ref, gain_ref, router_ref, up_ref, down_ref, outs, x_store,
                 der_store, hid_store, gate_store, nrm, hid, der, gates, sems, up_wait, down_wait):
    a0 = blocks[0]
    rows = a0.shape[1]
    total = SIDE * rows
    width, ff = up_ref.shape
    micro_idx = idx_ref[0]

    saves = [
        pltpu.make_async_copy(a0.at[0], x_store.at[micro_idx], sems.at[0]),
        pltpu.make_async_copy(der, der_store.at[micro_idx], sems.at[1]),
        pltpu.make_async_copy(hid.at[pl.ds(0, total)], hid_store.at[micro_idx], sems.at[2]),
        pltpu.make_async_copy(gates, gate_store.at[micro_idx], sems.at[3]),
    ]

    saves[0].start()
    gain = gain_ref[...]
    for d, a in enumerate(blocks):
        x = a[0].astype(F32)
        t = a[1].astype(F32)
        scale = lax.rsqrt(jnp.mean(x * x, axis=-1, keepdims=True) + norm_eps)
        moment = jnp.mean(x * t, axis=-1, keepdims=True)
        nrm[pl.ds(d * rows, rows), :] = (x * scale * gain).astype(BF)
        nrm[pl.ds(total + d * rows, rows), :] = (
            gain * (t * scale - x * (scale * scale * scale) * moment)
        ).astype(BF)
    logits = jnp.dot(nrm[...], router_ref[...], preferred_element_type=F32)
    contrast = c_ref[micro_idx]
    lane = lax.broadcasted_iota(jnp.int32, contrast.shape, 1)
    side = jnp.sum(jnp.where(lane == idx_ref[1], contrast, 0.0), axis=1, keepdims=True)
    margin = jnp.sum(logits[:total] * contrast, axis=1, keepdims=True)
    move = jnp.sum(logits[total:] * contrast, axis=1, keepdims=True)
    first = jax.nn.sigmoid(margin)
    slope = first * (1.0 - first)
    gate = jnp.where(side > 0.5, first, jnp.where(side < -0.5, 1.0 - first, 0.0))
    gates[0] = jnp.broadcast_to(gate, contrast.shape)
    gates[1] = jnp.broadcast_to(side * slope, contrast.shape)
    gates[2] = jnp.broadcast_to(side * slope * move, contrast.shape)
    saves[3].start()

    @pl.loop(0, ff // CHUNK)
    def _(chunk):
        up_wait(chunk)

        @pl.loop(0, CHUNK // TILE)
        def _(tile):
            span = pl.ds(pl.multiple_of(chunk * CHUNK + tile * TILE, TILE), TILE)
            pre_all = jnp.dot(nrm[...], up_ref[:, span], preferred_element_type=F32)
            pre = pre_all[:total]
            logistic = jax.nn.sigmoid(pre)
            derivative = logistic * (1.0 + pre * (1.0 - logistic))
            der[:, span] = derivative
            hid[pl.ds(0, total), span] = (pre * logistic).astype(BF)
            hid[pl.ds(total, total), span] = (derivative * pre_all[total:]).astype(BF)

    saves[1].start()
    saves[2].start()
    gate = gates[0, :, 0:1]
    shift = gates[2, :, 0:1]

    @pl.loop(0, width // CHUNK)
    def _(chunk):
        down_wait(chunk)

        @pl.loop(0, CHUNK // TILE)
        def _(tile):
            span = pl.ds(pl.multiple_of(chunk * CHUNK + tile * TILE, TILE), TILE)
            both = jnp.dot(hid[...], down_ref[:, span], preferred_element_type=F32)
            main = (gate * both[:total]).astype(BF)
            moved = (shift * both[:total] + gate * both[total:]).astype(BF)
            for d, o in enumerate(outs):
                o[0, :, span] = main[d * rows:(d + 1) * rows]
                o[1, :, span] = moved[d * rows:(d + 1) * rows]

    for save in saves:
        save.wait()


def backward_kernel(idx_ref, b0, b1, b2, b3, c_ref, router_ref, up_hbm, down_hbm, x_store,
                    der_store, hid_store, gate_store, o0, o1, o2, o3, x_ref, cot, back_hid, hid,
                    der, gates, up_ref, down_ref, sems, up_sems, down_sems):
    rows = b0.shape[1]
    total = SIDE * rows
    width, ff = up_ref.shape
    micro_idx = idx_ref[0]
    slot = idx_ref[2]

    def up_copy(j):
        span = pl.ds(pl.multiple_of(j * CHUNK, CHUNK), CHUNK)
        return pltpu.make_async_copy(up_hbm.at[span, :], up_ref.at[span, :], up_sems.at[j])

    def down_copy(j):
        span = pl.ds(pl.multiple_of(j * CHUNK, CHUNK), CHUNK)
        return pltpu.make_async_copy(down_hbm.at[span, :], down_ref.at[span, :], down_sems.at[j])

    loads = [
        pltpu.make_async_copy(der_store.at[micro_idx], der, sems.at[0]),
        pltpu.make_async_copy(hid_store.at[micro_idx], hid, sems.at[1]),
        pltpu.make_async_copy(gate_store.at[micro_idx], gates, sems.at[2]),
        pltpu.make_async_copy(x_store.at[micro_idx], x_ref, sems.at[3]),
    ]

    for load in loads:
        load.start()

    @pl.loop(0, ff // CHUNK)
    def _(j):
        down_copy(j).start()

    @pl.loop(0, width // CHUNK)
    def _(j):
        up_copy(j).start()

    @pl.loop(0, width // CHUNK)
    def _(j):
        span = pl.ds(pl.multiple_of(j * CHUNK, CHUNK), CHUNK)
        part = jnp.concatenate([b[slot, :, span] for b in (b0, b1, b2, b3)] * 2, axis=0)
        cot[span, :] = part.T
    for load in loads:
        load.wait()

    def hidden_step(chunk, pull):
        down_copy(chunk).wait()

        def tile_step(tile, pull):
            span = pl.ds(pl.multiple_of(chunk * CHUNK + tile * TILE, TILE), TILE)
            back = jnp.dot(down_ref[span, :], cot[...], preferred_element_type=F32)
            value = hid[:, span].astype(F32)
            both = jnp.concatenate([der[:, span], value], axis=0).T * back
            back_hid[span, :] = both.astype(BF)
            return pull + jnp.sum(both, axis=0, keepdims=True)

        return lax.fori_loop(0, CHUNK // TILE, tile_step, pull)

    pull = lax.fori_loop(0, ff // CHUNK, hidden_step, jnp.zeros((1, 2 * total), F32))
    pull = jnp.broadcast_to(pull, (LANES, 2 * total)).T[total:, 0:1]
    gate = gates[0, :, 0:1]
    grad = gates[1, :, 0:1] * pull
    contrast = c_ref[micro_idx].astype(BF)

    @pl.loop(0, width // CHUNK)
    def _(chunk):
        up_copy(chunk).wait()

        @pl.loop(0, CHUNK // TILE)
        def _(tile):
            span = pl.ds(pl.multiple_of(chunk * CHUNK + tile * TILE, TILE), TILE)
            back = jnp.dot(up_ref[span, :], back_hid[...], preferred_element_type=F32).T[:total]
            gap = lax.dot_general(
                contrast, router_ref[span, :], (((1,), (1,)), ((), ())), preferred_element_type=F32
            )
            part = (gate * back + grad * gap).astype(BF)
            for d, o in enumerate((o0, o1, o2, o3)):
                o[:, span] = part[d * rows:(d + 1) * rows]


SMEM_SPEC = pl.BlockSpec(memory_space=pltpu.SMEM)
VMEM_SPEC = pl.BlockSpec(memory_space=pltpu.VMEM)
ANY_SPEC = pl.BlockSpec(memory_space=pl.ANY)
HBM_SPEC = pl.BlockSpec(memory_space=pltpu.HBM)


def run_forward(idx, blocks, contrast, gain, router, w_in, w_out, stores, loaded=False):
    _, rows, width = blocks[0].shape
    ff = w_in.shape[1]
    total = SIDE * rows
    block = jax.ShapeDtypeStruct((2, rows, width), BF)
    scratch = [
        pltpu.VMEM((2 * total, width), BF),
        pltpu.VMEM((2 * total, ff), BF),
        pltpu.VMEM((total, ff), F32),
        pltpu.VMEM((3, total, LANES), F32),
        pltpu.SemaphoreType.DMA((4,)),
    ]
    stream = [
        pltpu.VMEM(w_in.shape, BF),
        pltpu.VMEM(w_out.shape, BF),
        pltpu.SemaphoreType.DMA((ff // CHUNK,)),
        pltpu.SemaphoreType.DMA((width // CHUNK,)),
    ]
    weight_spec = VMEM_SPEC if loaded else ANY_SPEC
    out = pl.pallas_call(
        loaded_kernel if loaded else forward_kernel,
        out_shape=(block,) * 4 + tuple(jax.ShapeDtypeStruct(s.shape, s.dtype) for s in stores),
        in_specs=[SMEM_SPEC] + [VMEM_SPEC] * 7 + [weight_spec] * 2 + [HBM_SPEC] * 4,
        out_specs=[VMEM_SPEC] * 4 + [HBM_SPEC] * 4,
        scratch_shapes=scratch if loaded else scratch + stream,
        input_output_aliases={10: 4, 11: 5, 12: 6, 13: 7},
        compiler_params=pltpu.CompilerParams(
            vmem_limit_bytes=LOADED_VMEM if loaded else KERNEL_VMEM
        ),
        name="loaded_layer" if loaded else "forward_layer",
    )(idx, *blocks, contrast, gain, router, w_in, w_out, *stores)
    return out[:4], tuple(out[4:])


def load_kernel(flag_ref, up_hbm, down_hbm, up, down, sems):
    @pl.when(flag_ref[2] == 1)
    def _():
        loads = [
            pltpu.make_async_copy(up_hbm, up, sems.at[0]),
            pltpu.make_async_copy(down_hbm, down, sems.at[1]),
        ]
        for load in loads:
            load.start()
        for load in loads:
            load.wait()


def load_weights(idx, w_in, w_out):
    return pl.pallas_call(
        load_kernel,
        out_shape=(pltpu.VMEM(w_in.shape, w_in.dtype), pltpu.VMEM(w_out.shape, w_out.dtype)),
        in_specs=[SMEM_SPEC] + [ANY_SPEC] * 2,
        out_specs=[VMEM_SPEC] * 2,
        scratch_shapes=[pltpu.SemaphoreType.DMA((2,))],
        compiler_params=pltpu.CompilerParams(vmem_limit_bytes=2**20),
        cost_estimate=pl.CostEstimate(flops=0, bytes_accessed=4 * w_in.size, transcendentals=0),
        name="load_weights",
    )(idx, w_in, w_out)


def run_backward(idx, blocks, contrast, router, w_in, w_out, stores):
    _, rows, width = blocks[0].shape
    ff = w_in.shape[1]
    total = SIDE * rows
    block = jax.ShapeDtypeStruct((rows, width), BF)
    return pl.pallas_call(
        backward_kernel,
        out_shape=(block,) * 5,
        in_specs=[SMEM_SPEC] + [VMEM_SPEC] * 6 + [ANY_SPEC] * 6,
        out_specs=[VMEM_SPEC] * 5,
        scratch_shapes=[
            pltpu.VMEM((width, 2 * total), BF),
            pltpu.VMEM((ff, 2 * total), BF),
            pltpu.VMEM((total, ff), BF),
            pltpu.VMEM((total, ff), F32),
            pltpu.VMEM((3, total, LANES), F32),
            pltpu.VMEM(w_in.shape, BF),
            pltpu.VMEM(w_out.shape, BF),
            pltpu.SemaphoreType.DMA((4,)),
            pltpu.SemaphoreType.DMA((width // CHUNK,)),
            pltpu.SemaphoreType.DMA((ff // CHUNK,)),
        ],
        compiler_params=pltpu.CompilerParams(vmem_limit_bytes=KERNEL_VMEM),
        name="backward_layer",
    )(idx, *blocks, contrast, router, w_in, w_out, *stores)


def forward_finish(block_ref, m0, m1, m2, m3, out_ref):
    moved = m0[...].astype(F32) + m1[...].astype(F32) + m2[...].astype(F32) + m3[...].astype(F32)
    out_ref[...] = (block_ref[...].astype(F32) + moved).astype(BF)


def backward_finish(idx_ref, block_ref, x_ref, gain_ref, m0, m1, m2, m3, out_ref):
    moved = m0[...].astype(F32) + m1[...].astype(F32) + m2[...].astype(F32) + m3[...].astype(F32)
    wide = x_ref[...].astype(F32)
    scale = lax.rsqrt(jnp.mean(wide * wide, axis=-1, keepdims=True) + norm_eps)
    weighted = gain_ref[...] * moved
    moment = jnp.mean(wide * weighted, axis=-1, keepdims=True)
    block = block_ref[idx_ref[2]].astype(F32)
    result = block + scale * weighted - wide * (scale * scale * scale) * moment
    for slot in range(out_ref.shape[0]):
        out_ref[slot] = result.astype(BF)


def run_finish(kernel, name, scalars, *operands):
    block = operands[0]
    return pl.pallas_call(
        kernel,
        out_shape=jax.ShapeDtypeStruct(block.shape, block.dtype),
        in_specs=[SMEM_SPEC] * len(scalars) + [VMEM_SPEC] * len(operands),
        out_specs=VMEM_SPEC,
        compiler_params=pltpu.CompilerParams(vmem_limit_bytes=8 * 2**20),
        name=name,
    )(*scalars, *operands)


def unset(*leaves):
    return pl.pallas_call(
        lambda *refs: None,
        out_shape=tuple(jax.ShapeDtypeStruct(shape, kind) for shape, kind in leaves),
        out_specs=(ANY_SPEC,) * len(leaves),
        name="unset",
    )()


def shards(tokens, tangent, w_up, w_down, w_router, norm_gain, route_ids):
    micro_count, tok_width, width = tokens.shape
    pipe_count = lax.axis_size("pipe")
    section = lax.axis_index("pipe")
    rank = lax.axis_index("expert")
    expert_y = rank // SIDE
    place_z = rank % SIDE
    w_in = w_up[0]
    w_out = w_down[0]
    gain = norm_gain
    router = jnp.pad(w_router[0], ((0, 0), (0, LANES - EXPERTS)))
    ff = w_in.shape[1]
    rows = SIDE * tok_width
    total = SIDE * rows

    ids = route_ids[0].reshape(micro_count, SIDE, SIDE, tok_width, 2)
    ids = ids.transpose(0, 2, 1, 3, 4).reshape(micro_count, SIDE, rows, 2)
    relative = (place_z - jnp.arange(SIDE)) % SIDE
    ids = jnp.take(ids, relative, axis=1).reshape(micro_count, total, 2)
    lane = jnp.arange(LANES, dtype=jnp.int32)
    contrast = (ids[:, :, 0:1] == lane).astype(F32) - (ids[:, :, 1:2] == lane).astype(F32)
    contrast, router = lax.optimization_barrier((contrast, router))

    start = jnp.stack([tokens, tangent], axis=1)
    groups = [[SIDE * y + z for y in range(SIDE)] for z in range(SIDE)]
    start = lax.all_gather(start, "expert", axis=2, tiled=True, axis_index_groups=groups)

    def reduce_all(parts):
        got = [z_send(parts[4 - d], d) for d in (2, 1, 3)]
        mine = parts[0].astype(F32) + got[0].astype(F32) + got[1].astype(F32) + got[2].astype(F32)
        mine = mine.astype(BF)
        return [mine] + [y_send(mine, d) for d in (2, 1, 3)]

    def make_idx(micro_idx, slot):
        return jnp.stack([micro_idx, expert_y, slot]).astype(jnp.int32)

    def plan(step):
        micro_idx = step // 2
        active = (step >= 0) & (step % 2 == 0) & (micro_idx < micro_count)
        return active, jnp.clip(micro_idx, 0, micro_count - 1)

    def forward_plan(tick):
        return plan(tick - section)

    def backward_plan(tick):
        return plan(tick - (2 * pipe_count - 1 - section))

    def fresh(tick):
        micro_idx = jnp.clip((tick + 1) // 2, 0, micro_count - 1)
        return lax.dynamic_index_in_dim(start, micro_idx, 0, keepdims=False)

    last = section == pipe_count - 1

    def forward_run(micro_idx, blocks, stores):
        parts, stores = run_forward(
            make_idx(micro_idx, 0), blocks, contrast, gain, router, w_in, w_out, stores
        )
        out = run_finish(forward_finish, "forward_finish", (), blocks[0], *reduce_all(parts))
        return out, stores

    def backward_run(micro_idx, slot, blocks, stores):
        idx = make_idx(micro_idx, slot)
        *parts, inputs = run_backward(idx, blocks, contrast, router, w_in, w_out, stores)
        return run_finish(
            backward_finish, "backward_finish", (idx,), blocks[0], inputs, gain, *reduce_all(parts)
        )

    def backward_half(tick, blocks, stores):
        active, micro_idx = backward_plan(tick)

        def run(blocks, stores):
            return backward_run(micro_idx, 0, blocks, stores)

        return lax.cond(active, run, lambda blocks, stores: blocks[0], blocks, stores)

    def either_half(tick, blocks, stores):
        forward_active, forward_idx = forward_plan(tick)
        backward_active, backward_idx = backward_plan(tick)

        def rest(blocks, stores):
            return blocks[0], stores

        def forward(blocks, stores):
            return forward_run(forward_idx, blocks, stores)

        def backward(blocks, stores):
            slot = last.astype(jnp.int32)
            return backward_run(backward_idx, slot, blocks, stores), stores

        branch = jnp.where(forward_active, 1, jnp.where(backward_active, 2, 0))
        return lax.switch(branch, (rest, forward, backward), blocks, stores)

    def store_probe(tick, result, probe_store):
        active, micro_idx = backward_plan(tick)
        write_idx = jnp.where(active, micro_idx, micro_count)
        return lax.dynamic_update_index_in_dim(probe_store, result, write_idx, 0)

    *stores, probe_store = unset(
        ((36 * micro_count, rows, width), BF),
        ((7 * micro_count, total, ff), F32),
        ((14 * micro_count, total, ff), BF),
        ((36 * micro_count, 3, total, LANES), F32),
        ((10 * micro_count, rows, width), BF),
    )
    stores = tuple(stores)
    def forward_ticks(pair_idx, state):
        send, stores = state
        plans = []
        for parity in range(2):
            tick = 2 * pair_idx + parity
            active, micro_idx = forward_plan(tick)
            plans.append((make_idx(micro_idx, active), active, tick))
        send, plans = lax.optimization_barrier((send, plans))
        for parity in range(2):
            idx, active, tick = plans[parity]
            blocks = pipe_gather(send, FORWARD_HOPS[parity])
            weights = load_weights(idx, w_in, w_out)
            parts, stores = run_forward(
                idx, blocks, contrast, gain, router, *weights, stores, loaded=True
            )

            parts, active, tick = lax.optimization_barrier((parts, active, tick))

            def run(block, parts, tick):
                return run_finish(forward_finish, "forward_finish", (), block, *reduce_all(parts))

            def rest(block, parts, tick):
                return jnp.where(last, fresh(tick), block)

            send = lax.cond(active, run, rest, blocks[0], parts, tick)
        return send, stores

    def both_ticks(pair_idx, state):
        send, stores, probe_store = state
        for parity in range(2):
            tick = 2 * pair_idx + parity
            blocks = pipe_gather(send, SWAP_HOPS[parity])
            probe_store = store_probe(tick - 1, send[0], probe_store)
            send, stores = either_half(tick, blocks, stores)
        return send, stores, probe_store

    def backward_ticks(pair_idx, state):
        back, probe_store = state
        for parity in range(2):
            tick = 2 * pair_idx + parity
            blocks = pipe_gather(back, BACKWARD_HOPS[parity])
            probe_store = store_probe(tick - 1, back[0], probe_store)
            back = backward_half(tick, blocks, stores)
        return back, probe_store

    lead = pipe_count // 2
    turn = lead + micro_count - 1
    send, stores = lax.fori_loop(0, lead, forward_ticks, (start[0], stores))
    send, stores, probe_store = lax.fori_loop(lead, turn, both_ticks, (send, stores, probe_store))
    back = jnp.where(last, send[1], send[0])[None]
    back, probe_store = lax.fori_loop(
        turn, pipe_count + micro_count - 1, backward_ticks, (back, probe_store)
    )
    back = back[0]
    probe_store = store_probe(2 * pipe_count + 2 * micro_count - 3, back, probe_store)
    probes = probe_store[:micro_count].reshape(micro_count, SIDE, tok_width, width)
    probes = lax.dynamic_index_in_dim(probes, expert_y, 1, keepdims=False)
    return probes[None]


def solution(mesh):
    in_specs = (
        P(None, "expert", None),
        P(None, "expert", None),
        P("pipe", None, "expert"),
        P("pipe", "expert", None),
        P("pipe", None, None),
        P("pipe", None),
        P("pipe", None, None, None),
    )
    out_specs = P("pipe", None, "expert", None)
    return jax.shard_map(shards, mesh=mesh, in_specs=in_specs, out_specs=out_specs, check_vma=False)
```

```python
import jax
import jax.numpy as jnp
from jax import lax
from jax.experimental import pallas as pl
from jax.experimental.pallas import tpu as pltpu
from jax.sharding import PartitionSpec as P

EXPERTS = 4
SIDE = 4
LANES = 128
TILE = 512
CHUNK = 512
KERNEL_VMEM = 36 * 2**20
LOADED_VMEM = 24 * 2**20

norm_eps = 1e-05
BF = jnp.bfloat16
F32 = jnp.float32


def z_send(block, distance):
    route = [(4 * y + z, 4 * y + (z + distance) % 4) for y in range(4) for z in range(4)]
    return lax.ppermute(block, "expert", route)


def y_send(block, distance):
    route = [(4 * y + z, 4 * ((y + distance) % 4) + z) for y in range(4) for z in range(4)]
    return lax.ppermute(block, "expert", route)


def pipe_send(block, hops, distance):
    route = [
        (16 * p + 4 * y + z, 16 * q + 4 * y + (z + distance) % 4)
        for p, q in hops
        for y in range(4)
        for z in range(4)
    ]
    return lax.ppermute(block, ("pipe", "expert"), route)


def pipe_gather(block, hops):
    sent = {d: pipe_send(block, hops, d) for d in (2, 1, 3, 0)}
    return [sent[d] for d in range(SIDE)]


FORWARD_HOPS = (((7, 0), (1, 2), (3, 4), (5, 6)), ((0, 1), (2, 3), (4, 5), (6, 7)))
BACKWARD_HOPS = (((7, 7), (6, 5), (4, 3), (2, 1)), ((7, 6), (5, 4), (3, 2), (1, 0)))
SWAP_HOPS = (
    ((7, 7), (1, 2), (3, 4), (5, 6), (2, 1), (4, 3), (6, 5)),
    FORWARD_HOPS[1] + BACKWARD_HOPS[1],
)


def forward_kernel(idx_ref, a0, a1, a2, a3, c_ref, gain_ref, router_ref, up_hbm, down_hbm,
                   x_in, der_in, hid_in, gate_in, o0, o1, o2, o3, x_store, der_store, hid_store,
                   gate_store, nrm, hid, der, gates, sems, up_ref, down_ref, up_sems, down_sems):
    _, ff = up_ref.shape
    width = down_ref.shape[1]

    def up_copy(j):
        span = pl.ds(pl.multiple_of(j * CHUNK, CHUNK), CHUNK)
        return pltpu.make_async_copy(up_hbm.at[:, span], up_ref.at[:, span], up_sems.at[j])

    def down_copy(j):
        span = pl.ds(pl.multiple_of(j * CHUNK, CHUNK), CHUNK)
        return pltpu.make_async_copy(down_hbm.at[:, span], down_ref.at[:, span], down_sems.at[j])

    @pl.loop(0, ff // CHUNK)
    def _(j):
        up_copy(j).start()

    @pl.loop(0, width // CHUNK)
    def _(j):
        down_copy(j).start()

    forward_body(idx_ref, (a0, a1, a2, a3), c_ref, gain_ref, router_ref, up_ref, down_ref,
                 (o0, o1, o2, o3), x_store, der_store, hid_store, gate_store, nrm, hid, der, gates,
                 sems, lambda j: up_copy(j).wait(), lambda j: down_copy(j).wait())


def loaded_kernel(idx_ref, a0, a1, a2, a3, c_ref, gain_ref, router_ref, up_ref, down_ref,
                  x_in, der_in, hid_in, gate_in, o0, o1, o2, o3, x_store, der_store, hid_store,
                  gate_store, nrm, hid, der, gates, sems):
    @pl.when(idx_ref[2] == 1)
    def _():
        forward_body(idx_ref, (a0, a1, a2, a3), c_ref, gain_ref, router_ref, up_ref, down_ref,
                     (o0, o1, o2, o3), x_store, der_store, hid_store, gate_store, nrm, hid, der,
                     gates, sems, lambda j: None, lambda j: None)


def forward_body(idx_ref, blocks, c_ref, gain_ref, router_ref, up_ref, down_ref, outs, x_store,
                 der_store, hid_store, gate_store, nrm, hid, der, gates, sems, up_wait, down_wait):
    a0 = blocks[0]
    rows = a0.shape[1]
    total = SIDE * rows
    width, ff = up_ref.shape
    micro_idx = idx_ref[0]

    saves = [
        pltpu.make_async_copy(a0.at[0], x_store.at[micro_idx], sems.at[0]),
        pltpu.make_async_copy(der, der_store.at[micro_idx], sems.at[1]),
        pltpu.make_async_copy(hid.at[pl.ds(0, total)], hid_store.at[micro_idx], sems.at[2]),
        pltpu.make_async_copy(gates, gate_store.at[micro_idx], sems.at[3]),
    ]

    saves[0].start()
    gain = gain_ref[...]
    for d, a in enumerate(blocks):
        x = a[0].astype(F32)
        t = a[1].astype(F32)
        scale = lax.rsqrt(jnp.mean(x * x, axis=-1, keepdims=True) + norm_eps)
        moment = jnp.mean(x * t, axis=-1, keepdims=True)
        nrm[pl.ds(d * rows, rows), :] = (x * scale * gain).astype(BF)
        nrm[pl.ds(total + d * rows, rows), :] = (
            gain * (t * scale - x * (scale * scale * scale) * moment)
        ).astype(BF)
    logits = jnp.dot(nrm[...], router_ref[...], preferred_element_type=F32)
    contrast = c_ref[micro_idx]
    lane = lax.broadcasted_iota(jnp.int32, contrast.shape, 1)
    side = jnp.sum(jnp.where(lane == idx_ref[1], contrast, 0.0), axis=1, keepdims=True)
    margin = jnp.sum(logits[:total] * contrast, axis=1, keepdims=True)
    move = jnp.sum(logits[total:] * contrast, axis=1, keepdims=True)
    first = jax.nn.sigmoid(margin)
    slope = first * (1.0 - first)
    gate = jnp.where(side > 0.5, first, jnp.where(side < -0.5, 1.0 - first, 0.0))
    gates[0] = jnp.broadcast_to(gate, contrast.shape)
    gates[1] = jnp.broadcast_to(side * slope, contrast.shape)
    gates[2] = jnp.broadcast_to(side * slope * move, contrast.shape)
    saves[3].start()

    @pl.loop(0, ff // CHUNK)
    def _(chunk):
        up_wait(chunk)

        @pl.loop(0, CHUNK // TILE)
        def _(tile):
            span = pl.ds(pl.multiple_of(chunk * CHUNK + tile * TILE, TILE), TILE)
            pre_all = jnp.dot(nrm[...], up_ref[:, span], preferred_element_type=F32)
            pre = pre_all[:total]
            logistic = jax.nn.sigmoid(pre)
            derivative = logistic * (1.0 + pre * (1.0 - logistic))
            der[:, span] = derivative
            hid[pl.ds(0, total), span] = (pre * logistic).astype(BF)
            hid[pl.ds(total, total), span] = (derivative * pre_all[total:]).astype(BF)

    saves[1].start()
    saves[2].start()
    gate = gates[0, :, 0:1]
    shift = gates[2, :, 0:1]

    @pl.loop(0, width // CHUNK)
    def _(chunk):
        down_wait(chunk)

        @pl.loop(0, CHUNK // TILE)
        def _(tile):
            span = pl.ds(pl.multiple_of(chunk * CHUNK + tile * TILE, TILE), TILE)
            both = jnp.dot(hid[...], down_ref[:, span], preferred_element_type=F32)
            main = (gate * both[:total]).astype(BF)
            moved = (shift * both[:total] + gate * both[total:]).astype(BF)
            for d, o in enumerate(outs):
                o[0, :, span] = main[d * rows:(d + 1) * rows]
                o[1, :, span] = moved[d * rows:(d + 1) * rows]

    for save in saves:
        save.wait()


def backward_kernel(idx_ref, b0, b1, b2, b3, c_ref, router_ref, up_hbm, down_hbm, x_store,
                    der_store, hid_store, gate_store, o0, o1, o2, o3, x_ref, cot, back_hid, hid,
                    der, gates, up_ref, down_ref, sems, up_sems, down_sems):
    rows = b0.shape[1]
    total = SIDE * rows
    width, ff = up_ref.shape
    micro_idx = idx_ref[0]
    slot = idx_ref[2]

    def up_copy(j):
        span = pl.ds(pl.multiple_of(j * CHUNK, CHUNK), CHUNK)
        return pltpu.make_async_copy(up_hbm.at[span, :], up_ref.at[span, :], up_sems.at[j])

    def down_copy(j):
        span = pl.ds(pl.multiple_of(j * CHUNK, CHUNK), CHUNK)
        return pltpu.make_async_copy(down_hbm.at[span, :], down_ref.at[span, :], down_sems.at[j])

    loads = [
        pltpu.make_async_copy(der_store.at[micro_idx], der, sems.at[0]),
        pltpu.make_async_copy(hid_store.at[micro_idx], hid, sems.at[1]),
        pltpu.make_async_copy(gate_store.at[micro_idx], gates, sems.at[2]),
        pltpu.make_async_copy(x_store.at[micro_idx], x_ref, sems.at[3]),
    ]

    for load in loads:
        load.start()

    @pl.loop(0, ff // CHUNK)
    def _(j):
        down_copy(j).start()

    @pl.loop(0, width // CHUNK)
    def _(j):
        up_copy(j).start()

    @pl.loop(0, width // CHUNK)
    def _(j):
        span = pl.ds(pl.multiple_of(j * CHUNK, CHUNK), CHUNK)
        part = jnp.concatenate([b[slot, :, span] for b in (b0, b1, b2, b3)] * 2, axis=0)
        cot[span, :] = part.T
    for load in loads:
        load.wait()

    def hidden_step(chunk, pull):
        down_copy(chunk).wait()

        def tile_step(tile, pull):
            span = pl.ds(pl.multiple_of(chunk * CHUNK + tile * TILE, TILE), TILE)
            back = jnp.dot(down_ref[span, :], cot[...], preferred_element_type=F32)
            value = hid[:, span].astype(F32)
            both = jnp.concatenate([der[:, span], value], axis=0).T * back
            back_hid[span, :] = both.astype(BF)
            return pull + jnp.sum(both, axis=0, keepdims=True)

        return lax.fori_loop(0, CHUNK // TILE, tile_step, pull)

    pull = lax.fori_loop(0, ff // CHUNK, hidden_step, jnp.zeros((1, 2 * total), F32))
    pull = jnp.broadcast_to(pull, (LANES, 2 * total)).T[total:, 0:1]
    gate = gates[0, :, 0:1]
    grad = gates[1, :, 0:1] * pull
    contrast = c_ref[micro_idx].astype(BF)

    @pl.loop(0, width // CHUNK)
    def _(chunk):
        up_copy(chunk).wait()

        @pl.loop(0, CHUNK // TILE)
        def _(tile):
            span = pl.ds(pl.multiple_of(chunk * CHUNK + tile * TILE, TILE), TILE)
            back = jnp.dot(up_ref[span, :], back_hid[...], preferred_element_type=F32).T[:total]
            gap = lax.dot_general(
                contrast, router_ref[span, :], (((1,), (1,)), ((), ())), preferred_element_type=F32
            )
            part = (gate * back + grad * gap).astype(BF)
            for d, o in enumerate((o0, o1, o2, o3)):
                o[:, span] = part[d * rows:(d + 1) * rows]


def turned_kernel(idx_ref, b0, b1, b2, b3, c_ref, router_ref, up_ref, down_ref, x_store,
                  der_store, hid_store, gate_store, o0, o1, o2, o3, x_ref, cot, back_hid, hid, der,
                  gates, sems):
    rows = b0.shape[1]
    total = SIDE * rows
    ff, width = up_ref.shape
    micro_idx = idx_ref[0]

    @pl.when(idx_ref[2] == 1)
    def _():
        loads = [
            pltpu.make_async_copy(der_store.at[micro_idx], der, sems.at[0]),
            pltpu.make_async_copy(hid_store.at[micro_idx], hid, sems.at[1]),
            pltpu.make_async_copy(gate_store.at[micro_idx], gates, sems.at[2]),
            pltpu.make_async_copy(x_store.at[micro_idx], x_ref, sems.at[3]),
        ]
        for load in loads:
            load.start()
        for d, b in enumerate((b0, b1, b2, b3)):
            cot[pl.ds(d * rows, rows), :] = b[0]
        for load in loads:
            load.wait()

        def tile_step(tile, pull):
            span = pl.ds(pl.multiple_of(tile * TILE, TILE), TILE)
            back = jnp.dot(cot[...], down_ref[:, span], preferred_element_type=F32)
            back_hid[:, span] = (der[:, span] * back).astype(BF)
            return pull + jnp.sum(back * hid[:, span].astype(F32), axis=1, keepdims=True)

        pull = lax.fori_loop(0, ff // TILE, tile_step, jnp.zeros((total, 1), F32))
        gate = gates[0, :, 0:1]
        grad = gates[1, :, 0:1] * pull
        contrast = c_ref[micro_idx].astype(BF)

        @pl.loop(0, width // TILE)
        def _(tile):
            span = pl.ds(pl.multiple_of(tile * TILE, TILE), TILE)
            back = jnp.dot(back_hid[...], up_ref[:, span], preferred_element_type=F32)
            gap = lax.dot_general(
                contrast, router_ref[span, :], (((1,), (1,)), ((), ())), preferred_element_type=F32
            )
            part = (gate * back + grad * gap).astype(BF)
            for d, o in enumerate((o0, o1, o2, o3)):
                o[0, :, span] = part[d * rows:(d + 1) * rows]


def turn_kernel(idx_ref, up_hbm, down_hbm, up, down, up_rows, down_rows, up_sems, down_sems):
    width, ff = up_hbm.shape

    def up_copy(j):
        span = pl.ds(pl.multiple_of(j * CHUNK, CHUNK), CHUNK)
        return pltpu.make_async_copy(up_hbm.at[span, :], up_rows.at[j % 2], up_sems.at[j % 2])

    def down_copy(j):
        span = pl.ds(pl.multiple_of(j * CHUNK, CHUNK), CHUNK)
        return pltpu.make_async_copy(down_hbm.at[span, :], down_rows.at[j % 2], down_sems.at[j % 2])

    def turn(copy, rows, out, chunks, columns):
        copy(0).start()

        @pl.loop(0, chunks)
        def _(j):
            @pl.when(j + 1 < chunks)
            def _():
                copy(j + 1).start()

            copy(j).wait()

            @pl.loop(0, columns // LANES)
            def _(i):
                piece = pl.ds(pl.multiple_of(i * LANES, LANES), LANES)
                span = pl.ds(pl.multiple_of(j * CHUNK, CHUNK), CHUNK)
                out[piece, span] = rows[j % 2, :, piece].T

    @pl.when(idx_ref[2] == 1)
    def _():
        turn(down_copy, down_rows, down, ff // CHUNK, width)
        turn(up_copy, up_rows, up, width // CHUNK, ff)


SMEM_SPEC = pl.BlockSpec(memory_space=pltpu.SMEM)
VMEM_SPEC = pl.BlockSpec(memory_space=pltpu.VMEM)
ANY_SPEC = pl.BlockSpec(memory_space=pl.ANY)
HBM_SPEC = pl.BlockSpec(memory_space=pltpu.HBM)


def run_forward(idx, blocks, contrast, gain, router, w_in, w_out, stores, loaded=False):
    _, rows, width = blocks[0].shape
    ff = w_in.shape[1]
    total = SIDE * rows
    block = jax.ShapeDtypeStruct((2, rows, width), BF)
    scratch = [
        pltpu.VMEM((2 * total, width), BF),
        pltpu.VMEM((2 * total, ff), BF),
        pltpu.VMEM((total, ff), F32),
        pltpu.VMEM((3, total, LANES), F32),
        pltpu.SemaphoreType.DMA((4,)),
    ]
    stream = [
        pltpu.VMEM(w_in.shape, BF),
        pltpu.VMEM(w_out.shape, BF),
        pltpu.SemaphoreType.DMA((ff // CHUNK,)),
        pltpu.SemaphoreType.DMA((width // CHUNK,)),
    ]
    weight_spec = VMEM_SPEC if loaded else ANY_SPEC
    out = pl.pallas_call(
        loaded_kernel if loaded else forward_kernel,
        out_shape=(block,) * 4 + tuple(jax.ShapeDtypeStruct(s.shape, s.dtype) for s in stores),
        in_specs=[SMEM_SPEC] + [VMEM_SPEC] * 7 + [weight_spec] * 2 + [HBM_SPEC] * 4,
        out_specs=[VMEM_SPEC] * 4 + [HBM_SPEC] * 4,
        scratch_shapes=scratch if loaded else scratch + stream,
        input_output_aliases={10: 4, 11: 5, 12: 6, 13: 7},
        compiler_params=pltpu.CompilerParams(
            vmem_limit_bytes=LOADED_VMEM if loaded else KERNEL_VMEM
        ),
        name="loaded_layer" if loaded else "forward_layer",
    )(idx, *blocks, contrast, gain, router, w_in, w_out, *stores)
    return out[:4], tuple(out[4:])


def load_kernel(flag_ref, up_hbm, down_hbm, up, down, sems):
    @pl.when(flag_ref[2] == 1)
    def _():
        loads = [
            pltpu.make_async_copy(up_hbm, up, sems.at[0]),
            pltpu.make_async_copy(down_hbm, down, sems.at[1]),
        ]
        for load in loads:
            load.start()
        for load in loads:
            load.wait()


def load_weights(idx, w_in, w_out):
    return pl.pallas_call(
        load_kernel,
        out_shape=(pltpu.VMEM(w_in.shape, w_in.dtype), pltpu.VMEM(w_out.shape, w_out.dtype)),
        in_specs=[SMEM_SPEC] + [ANY_SPEC] * 2,
        out_specs=[VMEM_SPEC] * 2,
        scratch_shapes=[pltpu.SemaphoreType.DMA((2,))],
        compiler_params=pltpu.CompilerParams(vmem_limit_bytes=2**20),
        cost_estimate=pl.CostEstimate(flops=0, bytes_accessed=4 * w_in.size, transcendentals=0),
        name="load_weights",
    )(idx, w_in, w_out)


def run_backward(idx, blocks, contrast, router, w_in, w_out, stores):
    _, rows, width = blocks[0].shape
    ff = w_in.shape[1]
    total = SIDE * rows
    block = jax.ShapeDtypeStruct((rows, width), BF)
    return pl.pallas_call(
        backward_kernel,
        out_shape=(block,) * 5,
        in_specs=[SMEM_SPEC] + [VMEM_SPEC] * 6 + [ANY_SPEC] * 6,
        out_specs=[VMEM_SPEC] * 5,
        scratch_shapes=[
            pltpu.VMEM((width, 2 * total), BF),
            pltpu.VMEM((ff, 2 * total), BF),
            pltpu.VMEM((total, ff), BF),
            pltpu.VMEM((total, ff), F32),
            pltpu.VMEM((3, total, LANES), F32),
            pltpu.VMEM(w_in.shape, BF),
            pltpu.VMEM(w_out.shape, BF),
            pltpu.SemaphoreType.DMA((4,)),
            pltpu.SemaphoreType.DMA((width // CHUNK,)),
            pltpu.SemaphoreType.DMA((ff // CHUNK,)),
        ],
        compiler_params=pltpu.CompilerParams(vmem_limit_bytes=KERNEL_VMEM),
        name="backward_layer",
    )(idx, *blocks, contrast, router, w_in, w_out, *stores)


def run_turned(idx, blocks, contrast, router, w_in, w_out, stores):
    _, rows, width = blocks[0].shape
    ff = w_in.shape[0]
    total = SIDE * rows
    block = jax.ShapeDtypeStruct((1, rows, width), BF)
    return pl.pallas_call(
        turned_kernel,
        out_shape=(block,) * 4 + (jax.ShapeDtypeStruct((rows, width), BF),),
        in_specs=[SMEM_SPEC] + [VMEM_SPEC] * 8 + [HBM_SPEC] * 4,
        out_specs=[VMEM_SPEC] * 5,
        scratch_shapes=[
            pltpu.VMEM((total, width), BF),
            pltpu.VMEM((total, ff), BF),
            pltpu.VMEM((total, ff), BF),
            pltpu.VMEM((total, ff), F32),
            pltpu.VMEM((3, total, LANES), F32),
            pltpu.SemaphoreType.DMA((4,)),
        ],
        compiler_params=pltpu.CompilerParams(vmem_limit_bytes=LOADED_VMEM),
        name="turned_layer",
    )(idx, *blocks, contrast, router, w_in, w_out, *stores)


def turn_weights(idx, w_in, w_out):
    width, ff = w_in.shape
    return pl.pallas_call(
        turn_kernel,
        out_shape=(pltpu.VMEM((ff, width), BF), pltpu.VMEM((width, ff), BF)),
        in_specs=[SMEM_SPEC] + [ANY_SPEC] * 2,
        out_specs=[VMEM_SPEC] * 2,
        scratch_shapes=[
            pltpu.VMEM((2, CHUNK, ff), BF),
            pltpu.VMEM((2, CHUNK, width), BF),
            pltpu.SemaphoreType.DMA((2,)),
            pltpu.SemaphoreType.DMA((2,)),
        ],
        compiler_params=pltpu.CompilerParams(vmem_limit_bytes=LOADED_VMEM),
        cost_estimate=pl.CostEstimate(flops=0, bytes_accessed=4 * w_in.size, transcendentals=0),
        name="turn_weights",
    )(idx, w_in, w_out)


def forward_finish(block_ref, m0, m1, m2, m3, out_ref):
    moved = m0[...].astype(F32) + m1[...].astype(F32) + m2[...].astype(F32) + m3[...].astype(F32)
    out_ref[...] = (block_ref[...].astype(F32) + moved).astype(BF)


def backward_finish(idx_ref, block_ref, x_ref, gain_ref, m0, m1, m2, m3, out_ref):
    moved = m0[...].astype(F32) + m1[...].astype(F32) + m2[...].astype(F32) + m3[...].astype(F32)
    wide = x_ref[...].astype(F32)
    scale = lax.rsqrt(jnp.mean(wide * wide, axis=-1, keepdims=True) + norm_eps)
    weighted = gain_ref[...] * moved
    moment = jnp.mean(wide * weighted, axis=-1, keepdims=True)
    block = block_ref[idx_ref[2]].astype(F32)
    result = block + scale * weighted - wide * (scale * scale * scale) * moment
    for slot in range(out_ref.shape[0]):
        out_ref[slot] = result.astype(BF)


def run_finish(kernel, name, scalars, *operands):
    block = operands[0]
    return pl.pallas_call(
        kernel,
        out_shape=jax.ShapeDtypeStruct(block.shape, block.dtype),
        in_specs=[SMEM_SPEC] * len(scalars) + [VMEM_SPEC] * len(operands),
        out_specs=VMEM_SPEC,
        compiler_params=pltpu.CompilerParams(vmem_limit_bytes=8 * 2**20),
        name=name,
    )(*scalars, *operands)


def unset(*leaves):
    return pl.pallas_call(
        lambda *refs: None,
        out_shape=tuple(jax.ShapeDtypeStruct(shape, kind) for shape, kind in leaves),
        out_specs=(ANY_SPEC,) * len(leaves),
        name="unset",
    )()


def shards(tokens, tangent, w_up, w_down, w_router, norm_gain, route_ids):
    micro_count, tok_width, width = tokens.shape
    pipe_count = lax.axis_size("pipe")
    section = lax.axis_index("pipe")
    rank = lax.axis_index("expert")
    expert_y = rank // SIDE
    place_z = rank % SIDE
    w_in = w_up[0]
    w_out = w_down[0]
    gain = norm_gain
    router = jnp.pad(w_router[0], ((0, 0), (0, LANES - EXPERTS)))
    ff = w_in.shape[1]
    rows = SIDE * tok_width
    total = SIDE * rows

    ids = route_ids[0].reshape(micro_count, SIDE, SIDE, tok_width, 2)
    ids = ids.transpose(0, 2, 1, 3, 4).reshape(micro_count, SIDE, rows, 2)
    relative = (place_z - jnp.arange(SIDE)) % SIDE
    ids = jnp.take(ids, relative, axis=1).reshape(micro_count, total, 2)
    lane = jnp.arange(LANES, dtype=jnp.int32)
    contrast = (ids[:, :, 0:1] == lane).astype(F32) - (ids[:, :, 1:2] == lane).astype(F32)
    contrast, router = lax.optimization_barrier((contrast, router))

    start = jnp.stack([tokens, tangent], axis=1)
    groups = [[SIDE * y + z for y in range(SIDE)] for z in range(SIDE)]
    start = lax.all_gather(start, "expert", axis=2, tiled=True, axis_index_groups=groups)

    def reduce_all(parts):
        got = [z_send(parts[4 - d], d) for d in (2, 1, 3)]
        mine = parts[0].astype(F32) + got[0].astype(F32) + got[1].astype(F32) + got[2].astype(F32)
        mine = mine.astype(BF)
        return [mine] + [y_send(mine, d) for d in (2, 1, 3)]

    def make_idx(micro_idx, slot):
        return jnp.stack([micro_idx, expert_y, slot]).astype(jnp.int32)

    def plan(step):
        micro_idx = step // 2
        active = (step >= 0) & (step % 2 == 0) & (micro_idx < micro_count)
        return active, jnp.clip(micro_idx, 0, micro_count - 1)

    def forward_plan(tick):
        return plan(tick - section)

    def backward_plan(tick):
        return plan(tick - (2 * pipe_count - 1 - section))

    def fresh(tick):
        micro_idx = jnp.clip((tick + 1) // 2, 0, micro_count - 1)
        return lax.dynamic_index_in_dim(start, micro_idx, 0, keepdims=False)

    last = section == pipe_count - 1

    def forward_run(micro_idx, blocks, stores):
        parts, stores = run_forward(
            make_idx(micro_idx, 0), blocks, contrast, gain, router, w_in, w_out, stores
        )
        out = run_finish(forward_finish, "forward_finish", (), blocks[0], *reduce_all(parts))
        return out, stores

    def backward_run(micro_idx, slot, blocks, stores):
        idx = make_idx(micro_idx, slot)
        *parts, inputs = run_backward(idx, blocks, contrast, router, w_in, w_out, stores)
        return run_finish(
            backward_finish, "backward_finish", (idx,), blocks[0], inputs, gain, *reduce_all(parts)
        )

    def either_half(tick, parity, blocks, stores):
        forward_active, forward_idx = forward_plan(tick)
        backward_active, backward_idx = backward_plan(tick)

        def rest(blocks, stores):
            return jnp.zeros_like(blocks[0]) if parity else blocks[0], stores

        def forward(blocks, stores):
            return forward_run(forward_idx, blocks, stores)

        def backward(blocks, stores):
            slot = last.astype(jnp.int32)
            return backward_run(backward_idx, slot, blocks, stores), stores

        branch = jnp.where(forward_active, 1, jnp.where(backward_active, 2, 0))
        return lax.switch(branch, (rest, forward, backward), blocks, stores)

    def store_probe(tick, result, probe_store):
        active, micro_idx = backward_plan(tick)
        write_idx = jnp.where(active, micro_idx, micro_count)
        return lax.dynamic_update_index_in_dim(probe_store, result, write_idx, 0)

    *stores, probe_store = unset(
        ((36 * micro_count, rows, width), BF),
        ((7 * micro_count, total, ff), F32),
        ((14 * micro_count, total, ff), BF),
        ((36 * micro_count, 3, total, LANES), F32),
        ((10 * micro_count, rows, width), BF),
    )
    stores = tuple(stores)
    def forward_ticks(pair_idx, state):
        send, stores = state
        plans = []
        for parity in range(2):
            tick = 2 * pair_idx + parity
            active, micro_idx = forward_plan(tick)
            plans.append((make_idx(micro_idx, active), active, tick))
        send, plans = lax.optimization_barrier((send, plans))
        for parity in range(2):
            idx, active, tick = plans[parity]
            blocks = pipe_gather(send, FORWARD_HOPS[parity])
            weights = load_weights(idx, w_in, w_out)
            parts, stores = run_forward(
                idx, blocks, contrast, gain, router, *weights, stores, loaded=True
            )

            parts, active, tick = lax.optimization_barrier((parts, active, tick))

            def run(block, parts, tick):
                return run_finish(forward_finish, "forward_finish", (), block, *reduce_all(parts))

            def rest(block, parts, tick):
                return jnp.where(last, fresh(tick), block)

            send = lax.cond(active, run, rest, blocks[0], parts, tick)
        return send, stores

    def both_ticks(pair_idx, state):
        send, stores, probe_store = state
        for parity in range(2):
            tick = 2 * pair_idx + parity
            blocks = pipe_gather(send, SWAP_HOPS[parity])
            probe_store = store_probe(tick - 1, send[0], probe_store)
            send, stores = either_half(tick, parity, blocks, stores)
        return send, stores, probe_store

    def backward_ticks(pair_idx, state):
        back, probe_store = state
        plans = []
        for parity in range(2):
            tick = 2 * pair_idx + parity
            active, micro_idx = backward_plan(tick)
            prior, prior_idx = backward_plan(tick - 1)
            write_idx = jnp.where(prior, prior_idx, micro_count)
            plans.append((make_idx(micro_idx, active), active, write_idx))
        back, plans = lax.optimization_barrier((back, plans))
        for parity in range(2):
            idx, active, write_idx = plans[parity]
            back, idx = lax.optimization_barrier((back, idx))
            result = back[0]
            blocks = pipe_gather(back, BACKWARD_HOPS[parity])
            weights = turn_weights(idx, w_in, w_out)
            *parts, inputs = run_turned(idx, blocks, contrast, router, *weights, stores)
            parts, inputs, active, write_idx = lax.optimization_barrier(
                (parts, inputs, active, write_idx)
            )

            def run(block, parts, inputs):
                return run_finish(
                    backward_finish, "backward_finish", (jnp.zeros((3,), jnp.int32),),
                    block, inputs, gain, *reduce_all([part[0] for part in parts])
                )

            back = lax.cond(active, run, lambda block, parts, inputs: block, blocks[0], parts, inputs)
            probe_store = lax.dynamic_update_index_in_dim(probe_store, result, write_idx, 0)
        return back, probe_store

    lead = pipe_count // 2
    turn = lead + micro_count - 1
    send, stores = lax.fori_loop(0, lead, forward_ticks, (start[0], stores))
    send, stores, probe_store = lax.fori_loop(lead, turn, both_ticks, (send, stores, probe_store))
    back = jnp.where(last, send[1], send[0])[None]
    back, probe_store = lax.fori_loop(
        turn, pipe_count + micro_count - 1, backward_ticks, (back, probe_store)
    )
    back = back[0]
    probe_store = store_probe(2 * pipe_count + 2 * micro_count - 3, back, probe_store)
    probes = probe_store[:micro_count].reshape(micro_count, SIDE, tok_width, width)
    probes = lax.dynamic_index_in_dim(probes, expert_y, 1, keepdims=False)
    return probes[None]


def solution(mesh):
    in_specs = (
        P(None, "expert", None),
        P(None, "expert", None),
        P("pipe", None, "expert"),
        P("pipe", "expert", None),
        P("pipe", None, None),
        P("pipe", None),
        P("pipe", None, None, None),
    )
    out_specs = P("pipe", None, "expert", None)
    return jax.shard_map(shards, mesh=mesh, in_specs=in_specs, out_specs=out_specs, check_vma=False)
```

```python
import jax
import jax.numpy as jnp
from jax import lax
from jax.experimental import pallas as pl
from jax.experimental.pallas import tpu as pltpu
from jax.sharding import PartitionSpec as P

EXPERTS = 4
SIDE = 4
LANES = 128
TILE = 512
CHUNK = 512
KERNEL_VMEM = 36 * 2**20
LOADED_VMEM = 24 * 2**20

norm_eps = 1e-05
BF = jnp.bfloat16
F32 = jnp.float32


def z_send(block, distance):
    route = [(4 * y + z, 4 * y + (z + distance) % 4) for y in range(4) for z in range(4)]
    return lax.ppermute(block, "expert", route)


def y_send(block, distance):
    route = [(4 * y + z, 4 * ((y + distance) % 4) + z) for y in range(4) for z in range(4)]
    return lax.ppermute(block, "expert", route)


def pipe_send(block, hops, distance):
    route = [
        (16 * p + 4 * y + z, 16 * q + 4 * y + (z + distance) % 4)
        for p, q in hops
        for y in range(4)
        for z in range(4)
    ]
    return lax.ppermute(block, ("pipe", "expert"), route)


def pipe_gather(block, hops):
    sent = {d: pipe_send(block, hops, d) for d in (2, 1, 3, 0)}
    return [sent[d] for d in range(SIDE)]


FORWARD_HOPS = (((7, 0), (1, 2), (3, 4), (5, 6)), ((0, 1), (2, 3), (4, 5), (6, 7)))
BACKWARD_HOPS = (((7, 7), (6, 5), (4, 3), (2, 1)), ((7, 6), (5, 4), (3, 2), (1, 0)))
SWAP_HOPS = (
    ((7, 7), (1, 2), (3, 4), (5, 6), (2, 1), (4, 3), (6, 5)),
    FORWARD_HOPS[1] + BACKWARD_HOPS[1],
)


def forward_kernel(idx_ref, a0, a1, a2, a3, c_ref, gain_ref, router_ref, up_hbm, down_hbm,
                   x_in, der_in, hid_in, gate_in, o0, o1, o2, o3, x_store, der_store, hid_store,
                   gate_store, nrm, hid, der, gates, sems, up_ref, down_ref, up_sems, down_sems):
    _, ff = up_ref.shape
    width = down_ref.shape[1]

    def up_copy(j):
        span = pl.ds(pl.multiple_of(j * CHUNK, CHUNK), CHUNK)
        return pltpu.make_async_copy(up_hbm.at[:, span], up_ref.at[:, span], up_sems.at[j])

    def down_copy(j):
        span = pl.ds(pl.multiple_of(j * CHUNK, CHUNK), CHUNK)
        return pltpu.make_async_copy(down_hbm.at[:, span], down_ref.at[:, span], down_sems.at[j])

    @pl.loop(0, ff // CHUNK)
    def _(j):
        up_copy(j).start()

    @pl.loop(0, width // CHUNK)
    def _(j):
        down_copy(j).start()

    forward_body(idx_ref, (a0, a1, a2, a3), c_ref, gain_ref, router_ref, up_ref, down_ref,
                 (o0, o1, o2, o3), x_store, der_store, hid_store, gate_store, nrm, hid, der, gates,
                 sems, lambda j: up_copy(j).wait(), lambda j: down_copy(j).wait())


def loaded_kernel(idx_ref, a0, a1, a2, a3, c_ref, gain_ref, router_ref, up_ref, down_ref,
                  x_in, der_in, hid_in, gate_in, o0, o1, o2, o3, x_store, der_store, hid_store,
                  gate_store, nrm, hid, der, gates, sems):
    @pl.when(idx_ref[2] == 1)
    def _():
        forward_body(idx_ref, (a0, a1, a2, a3), c_ref, gain_ref, router_ref, up_ref, down_ref,
                     (o0, o1, o2, o3), x_store, der_store, hid_store, gate_store, nrm, hid, der,
                     gates, sems, lambda j: None, lambda j: None)


def forward_body(idx_ref, blocks, c_ref, gain_ref, router_ref, up_ref, down_ref, outs, x_store,
                 der_store, hid_store, gate_store, nrm, hid, der, gates, sems, up_wait, down_wait):
    a0 = blocks[0]
    rows = a0.shape[1]
    total = SIDE * rows
    width, ff = up_ref.shape
    micro_idx = idx_ref[0]

    saves = [
        pltpu.make_async_copy(a0.at[0], x_store.at[micro_idx], sems.at[0]),
        pltpu.make_async_copy(der, der_store.at[micro_idx], sems.at[1]),
        pltpu.make_async_copy(hid.at[pl.ds(0, total)], hid_store.at[micro_idx], sems.at[2]),
        pltpu.make_async_copy(gates, gate_store.at[micro_idx], sems.at[3]),
    ]

    saves[0].start()
    gain = gain_ref[...]
    for d, a in enumerate(blocks):
        x = a[0].astype(F32)
        t = a[1].astype(F32)
        scale = lax.rsqrt(jnp.mean(x * x, axis=-1, keepdims=True) + norm_eps)
        moment = jnp.mean(x * t, axis=-1, keepdims=True)
        nrm[pl.ds(d * rows, rows), :] = (x * scale * gain).astype(BF)
        nrm[pl.ds(total + d * rows, rows), :] = (
            gain * (t * scale - x * (scale * scale * scale) * moment)
        ).astype(BF)
    logits = jnp.dot(nrm[...], router_ref[...], preferred_element_type=F32)
    contrast = c_ref[micro_idx]
    lane = lax.broadcasted_iota(jnp.int32, contrast.shape, 1)
    side = jnp.sum(jnp.where(lane == idx_ref[1], contrast, 0.0), axis=1, keepdims=True)
    margin = jnp.sum(logits[:total] * contrast, axis=1, keepdims=True)
    move = jnp.sum(logits[total:] * contrast, axis=1, keepdims=True)
    first = jax.nn.sigmoid(margin)
    slope = first * (1.0 - first)
    gate = jnp.where(side > 0.5, first, jnp.where(side < -0.5, 1.0 - first, 0.0))
    gates[0] = jnp.broadcast_to(gate, contrast.shape)
    gates[1] = jnp.broadcast_to(side * slope, contrast.shape)
    gates[2] = jnp.broadcast_to(side * slope * move, contrast.shape)
    saves[3].start()

    @pl.loop(0, ff // CHUNK)
    def _(chunk):
        up_wait(chunk)

        @pl.loop(0, CHUNK // TILE)
        def _(tile):
            span = pl.ds(pl.multiple_of(chunk * CHUNK + tile * TILE, TILE), TILE)
            pre_all = jnp.dot(nrm[...], up_ref[:, span], preferred_element_type=F32)
            pre = pre_all[:total]
            logistic = jax.nn.sigmoid(pre)
            derivative = logistic * (1.0 + pre * (1.0 - logistic))
            der[:, span] = derivative
            hid[pl.ds(0, total), span] = (pre * logistic).astype(BF)
            hid[pl.ds(total, total), span] = (derivative * pre_all[total:]).astype(BF)

    saves[1].start()
    saves[2].start()
    gate = gates[0, :, 0:1]
    shift = gates[2, :, 0:1]

    @pl.loop(0, width // CHUNK)
    def _(chunk):
        down_wait(chunk)

        @pl.loop(0, CHUNK // TILE)
        def _(tile):
            span = pl.ds(pl.multiple_of(chunk * CHUNK + tile * TILE, TILE), TILE)
            both = jnp.dot(hid[...], down_ref[:, span], preferred_element_type=F32)
            main = (gate * both[:total]).astype(BF)
            moved = (shift * both[:total] + gate * both[total:]).astype(BF)
            for d, o in enumerate(outs):
                o[0, :, span] = main[d * rows:(d + 1) * rows]
                o[1, :, span] = moved[d * rows:(d + 1) * rows]

    for save in saves:
        save.wait()


def backward_kernel(idx_ref, b0, b1, b2, b3, c_ref, router_ref, up_hbm, down_hbm, x_store,
                    der_store, hid_store, gate_store, o0, o1, o2, o3, x_ref, cot, back_hid, hid,
                    der, gates, up_ref, down_ref, sems, up_sems, down_sems):
    rows = b0.shape[1]
    total = SIDE * rows
    width, ff = up_ref.shape
    micro_idx = idx_ref[0]
    slot = idx_ref[2]

    def up_copy(j):
        span = pl.ds(pl.multiple_of(j * CHUNK, CHUNK), CHUNK)
        return pltpu.make_async_copy(up_hbm.at[span, :], up_ref.at[span, :], up_sems.at[j])

    def down_copy(j):
        span = pl.ds(pl.multiple_of(j * CHUNK, CHUNK), CHUNK)
        return pltpu.make_async_copy(down_hbm.at[span, :], down_ref.at[span, :], down_sems.at[j])

    loads = [
        pltpu.make_async_copy(der_store.at[micro_idx], der, sems.at[0]),
        pltpu.make_async_copy(hid_store.at[micro_idx], hid, sems.at[1]),
        pltpu.make_async_copy(gate_store.at[micro_idx], gates, sems.at[2]),
        pltpu.make_async_copy(x_store.at[micro_idx], x_ref, sems.at[3]),
    ]

    for load in loads:
        load.start()

    @pl.loop(0, ff // CHUNK)
    def _(j):
        down_copy(j).start()

    @pl.loop(0, width // CHUNK)
    def _(j):
        up_copy(j).start()

    @pl.loop(0, width // CHUNK)
    def _(j):
        span = pl.ds(pl.multiple_of(j * CHUNK, CHUNK), CHUNK)
        part = jnp.concatenate([b[slot, :, span] for b in (b0, b1, b2, b3)] * 2, axis=0)
        cot[span, :] = part.T

    def hidden_step(chunk, pull):
        down_copy(chunk).wait()

        def tile_step(tile, pull):
            span = pl.ds(pl.multiple_of(chunk * CHUNK + tile * TILE, TILE), TILE)
            back = jnp.dot(down_ref[span, :], cot[...], preferred_element_type=F32)

            @pl.when(chunk + tile == 0)
            def _():
                for load in loads:
                    load.wait()

            value = hid[:, span].astype(F32)
            both = jnp.concatenate([der[:, span], value], axis=0).T * back
            back_hid[span, :] = both.astype(BF)
            return pull + jnp.sum(both, axis=0, keepdims=True)

        return lax.fori_loop(0, CHUNK // TILE, tile_step, pull)

    pull = lax.fori_loop(0, ff // CHUNK, hidden_step, jnp.zeros((1, 2 * total), F32))
    pull = jnp.broadcast_to(pull, (LANES, 2 * total)).T[total:, 0:1]
    gate = gates[0, :, 0:1]
    grad = gates[1, :, 0:1] * pull
    contrast = c_ref[micro_idx].astype(BF)

    @pl.loop(0, width // CHUNK)
    def _(chunk):
        up_copy(chunk).wait()

        @pl.loop(0, CHUNK // TILE)
        def _(tile):
            span = pl.ds(pl.multiple_of(chunk * CHUNK + tile * TILE, TILE), TILE)
            back = jnp.dot(up_ref[span, :], back_hid[...], preferred_element_type=F32).T[:total]
            gap = lax.dot_general(
                contrast, router_ref[span, :], (((1,), (1,)), ((), ())), preferred_element_type=F32
            )
            part = (gate * back + grad * gap).astype(BF)
            for d, o in enumerate((o0, o1, o2, o3)):
                o[:, span] = part[d * rows:(d + 1) * rows]


def turned_kernel(idx_ref, b0, b1, b2, b3, c_ref, router_ref, up_ref, down_ref, x_store,
                  der_store, hid_store, gate_store, o0, o1, o2, o3, x_ref, cot, back_hid, hid, der,
                  gates, sems):
    rows = b0.shape[1]
    total = SIDE * rows
    ff, width = up_ref.shape
    micro_idx = idx_ref[0]

    @pl.when(idx_ref[2] == 1)
    def _():
        loads = [
            pltpu.make_async_copy(der_store.at[micro_idx], der, sems.at[0]),
            pltpu.make_async_copy(hid_store.at[micro_idx], hid, sems.at[1]),
            pltpu.make_async_copy(gate_store.at[micro_idx], gates, sems.at[2]),
            pltpu.make_async_copy(x_store.at[micro_idx], x_ref, sems.at[3]),
        ]
        for load in loads:
            load.start()
        for d, b in enumerate((b0, b1, b2, b3)):
            cot[pl.ds(d * rows, rows), :] = b[0]

        def tile_step(tile, pull):
            span = pl.ds(pl.multiple_of(tile * TILE, TILE), TILE)
            back = jnp.dot(cot[...], down_ref[:, span], preferred_element_type=F32)

            @pl.when(tile == 0)
            def _():
                for load in loads:
                    load.wait()

            back_hid[:, span] = (der[:, span] * back).astype(BF)
            return pull + jnp.sum(back * hid[:, span].astype(F32), axis=1, keepdims=True)

        pull = lax.fori_loop(0, ff // TILE, tile_step, jnp.zeros((total, 1), F32))
        gate = gates[0, :, 0:1]
        grad = gates[1, :, 0:1] * pull
        contrast = c_ref[micro_idx].astype(BF)

        @pl.loop(0, width // TILE)
        def _(tile):
            span = pl.ds(pl.multiple_of(tile * TILE, TILE), TILE)
            back = jnp.dot(back_hid[...], up_ref[:, span], preferred_element_type=F32)
            gap = lax.dot_general(
                contrast, router_ref[span, :], (((1,), (1,)), ((), ())), preferred_element_type=F32
            )
            part = (gate * back + grad * gap).astype(BF)
            for d, o in enumerate((o0, o1, o2, o3)):
                o[0, :, span] = part[d * rows:(d + 1) * rows]


def turn_kernel(idx_ref, up_hbm, down_hbm, up, down, up_rows, down_rows, up_sems, down_sems):
    width, ff = up_hbm.shape

    def up_copy(j):
        span = pl.ds(pl.multiple_of(j * CHUNK, CHUNK), CHUNK)
        return pltpu.make_async_copy(up_hbm.at[span, :], up_rows.at[j % 2], up_sems.at[j % 2])

    def down_copy(j):
        span = pl.ds(pl.multiple_of(j * CHUNK, CHUNK), CHUNK)
        return pltpu.make_async_copy(down_hbm.at[span, :], down_rows.at[j % 2], down_sems.at[j % 2])

    def turn(copy, rows, out, chunks, columns):
        copy(0).start()

        @pl.loop(0, chunks)
        def _(j):
            @pl.when(j + 1 < chunks)
            def _():
                copy(j + 1).start()

            copy(j).wait()

            @pl.loop(0, columns // LANES)
            def _(i):
                piece = pl.ds(pl.multiple_of(i * LANES, LANES), LANES)
                span = pl.ds(pl.multiple_of(j * CHUNK, CHUNK), CHUNK)
                out[piece, span] = rows[j % 2, :, piece].T

    @pl.when(idx_ref[2] == 1)
    def _():
        turn(down_copy, down_rows, down, ff // CHUNK, width)
        turn(up_copy, up_rows, up, width // CHUNK, ff)


SMEM_SPEC = pl.BlockSpec(memory_space=pltpu.SMEM)
VMEM_SPEC = pl.BlockSpec(memory_space=pltpu.VMEM)
ANY_SPEC = pl.BlockSpec(memory_space=pl.ANY)
HBM_SPEC = pl.BlockSpec(memory_space=pltpu.HBM)


def run_forward(idx, blocks, contrast, gain, router, w_in, w_out, stores, loaded=False):
    _, rows, width = blocks[0].shape
    ff = w_in.shape[1]
    total = SIDE * rows
    block = jax.ShapeDtypeStruct((2, rows, width), BF)
    scratch = [
        pltpu.VMEM((2 * total, width), BF),
        pltpu.VMEM((2 * total, ff), BF),
        pltpu.VMEM((total, ff), F32),
        pltpu.VMEM((3, total, LANES), F32),
        pltpu.SemaphoreType.DMA((4,)),
    ]
    stream = [
        pltpu.VMEM(w_in.shape, BF),
        pltpu.VMEM(w_out.shape, BF),
        pltpu.SemaphoreType.DMA((ff // CHUNK,)),
        pltpu.SemaphoreType.DMA((width // CHUNK,)),
    ]
    weight_spec = VMEM_SPEC if loaded else ANY_SPEC
    out = pl.pallas_call(
        loaded_kernel if loaded else forward_kernel,
        out_shape=(block,) * 4 + tuple(jax.ShapeDtypeStruct(s.shape, s.dtype) for s in stores),
        in_specs=[SMEM_SPEC] + [VMEM_SPEC] * 7 + [weight_spec] * 2 + [HBM_SPEC] * 4,
        out_specs=[VMEM_SPEC] * 4 + [HBM_SPEC] * 4,
        scratch_shapes=scratch if loaded else scratch + stream,
        input_output_aliases={10: 4, 11: 5, 12: 6, 13: 7},
        compiler_params=pltpu.CompilerParams(
            vmem_limit_bytes=LOADED_VMEM if loaded else KERNEL_VMEM
        ),
        name="loaded_layer" if loaded else "forward_layer",
    )(idx, *blocks, contrast, gain, router, w_in, w_out, *stores)
    return out[:4], tuple(out[4:])


def load_kernel(flag_ref, up_hbm, down_hbm, up, down, sems):
    @pl.when(flag_ref[2] == 1)
    def _():
        loads = [
            pltpu.make_async_copy(up_hbm, up, sems.at[0]),
            pltpu.make_async_copy(down_hbm, down, sems.at[1]),
        ]
        for load in loads:
            load.start()
        for load in loads:
            load.wait()


def load_weights(idx, w_in, w_out):
    return pl.pallas_call(
        load_kernel,
        out_shape=(pltpu.VMEM(w_in.shape, w_in.dtype), pltpu.VMEM(w_out.shape, w_out.dtype)),
        in_specs=[SMEM_SPEC] + [ANY_SPEC] * 2,
        out_specs=[VMEM_SPEC] * 2,
        scratch_shapes=[pltpu.SemaphoreType.DMA((2,))],
        compiler_params=pltpu.CompilerParams(vmem_limit_bytes=2**20),
        cost_estimate=pl.CostEstimate(flops=0, bytes_accessed=4 * w_in.size, transcendentals=0),
        name="load_weights",
    )(idx, w_in, w_out)


def run_backward(idx, blocks, contrast, router, w_in, w_out, stores):
    _, rows, width = blocks[0].shape
    ff = w_in.shape[1]
    total = SIDE * rows
    block = jax.ShapeDtypeStruct((rows, width), BF)
    return pl.pallas_call(
        backward_kernel,
        out_shape=(block,) * 5,
        in_specs=[SMEM_SPEC] + [VMEM_SPEC] * 6 + [ANY_SPEC] * 6,
        out_specs=[VMEM_SPEC] * 5,
        scratch_shapes=[
            pltpu.VMEM((width, 2 * total), BF),
            pltpu.VMEM((ff, 2 * total), BF),
            pltpu.VMEM((total, ff), BF),
            pltpu.VMEM((total, ff), F32),
            pltpu.VMEM((3, total, LANES), F32),
            pltpu.VMEM(w_in.shape, BF),
            pltpu.VMEM(w_out.shape, BF),
            pltpu.SemaphoreType.DMA((4,)),
            pltpu.SemaphoreType.DMA((width // CHUNK,)),
            pltpu.SemaphoreType.DMA((ff // CHUNK,)),
        ],
        compiler_params=pltpu.CompilerParams(vmem_limit_bytes=KERNEL_VMEM),
        name="backward_layer",
    )(idx, *blocks, contrast, router, w_in, w_out, *stores)


def run_turned(idx, blocks, contrast, router, w_in, w_out, stores):
    _, rows, width = blocks[0].shape
    ff = w_in.shape[0]
    total = SIDE * rows
    block = jax.ShapeDtypeStruct((1, rows, width), BF)
    return pl.pallas_call(
        turned_kernel,
        out_shape=(block,) * 4 + (jax.ShapeDtypeStruct((rows, width), BF),),
        in_specs=[SMEM_SPEC] + [VMEM_SPEC] * 8 + [HBM_SPEC] * 4,
        out_specs=[VMEM_SPEC] * 5,
        scratch_shapes=[
            pltpu.VMEM((total, width), BF),
            pltpu.VMEM((total, ff), BF),
            pltpu.VMEM((total, ff), BF),
            pltpu.VMEM((total, ff), F32),
            pltpu.VMEM((3, total, LANES), F32),
            pltpu.SemaphoreType.DMA((4,)),
        ],
        compiler_params=pltpu.CompilerParams(vmem_limit_bytes=LOADED_VMEM),
        name="turned_layer",
    )(idx, *blocks, contrast, router, w_in, w_out, *stores)


def turn_weights(idx, w_in, w_out):
    width, ff = w_in.shape
    return pl.pallas_call(
        turn_kernel,
        out_shape=(pltpu.VMEM((ff, width), BF), pltpu.VMEM((width, ff), BF)),
        in_specs=[SMEM_SPEC] + [ANY_SPEC] * 2,
        out_specs=[VMEM_SPEC] * 2,
        scratch_shapes=[
            pltpu.VMEM((2, CHUNK, ff), BF),
            pltpu.VMEM((2, CHUNK, width), BF),
            pltpu.SemaphoreType.DMA((2,)),
            pltpu.SemaphoreType.DMA((2,)),
        ],
        compiler_params=pltpu.CompilerParams(vmem_limit_bytes=LOADED_VMEM),
        cost_estimate=pl.CostEstimate(flops=0, bytes_accessed=4 * w_in.size, transcendentals=0),
        name="turn_weights",
    )(idx, w_in, w_out)


def forward_finish(block_ref, m0, m1, m2, m3, out_ref):
    moved = m0[...].astype(F32) + m1[...].astype(F32) + m2[...].astype(F32) + m3[...].astype(F32)
    out_ref[...] = (block_ref[...].astype(F32) + moved).astype(BF)


def backward_finish(idx_ref, block_ref, x_ref, gain_ref, m0, m1, m2, m3, out_ref):
    moved = m0[...].astype(F32) + m1[...].astype(F32) + m2[...].astype(F32) + m3[...].astype(F32)
    wide = x_ref[...].astype(F32)
    scale = lax.rsqrt(jnp.mean(wide * wide, axis=-1, keepdims=True) + norm_eps)
    weighted = gain_ref[...] * moved
    moment = jnp.mean(wide * weighted, axis=-1, keepdims=True)
    block = block_ref[idx_ref[2]].astype(F32)
    result = block + scale * weighted - wide * (scale * scale * scale) * moment
    for slot in range(out_ref.shape[0]):
        out_ref[slot] = result.astype(BF)


def run_finish(kernel, name, scalars, *operands):
    block = operands[0]
    return pl.pallas_call(
        kernel,
        out_shape=jax.ShapeDtypeStruct(block.shape, block.dtype),
        in_specs=[SMEM_SPEC] * len(scalars) + [VMEM_SPEC] * len(operands),
        out_specs=VMEM_SPEC,
        compiler_params=pltpu.CompilerParams(vmem_limit_bytes=8 * 2**20),
        name=name,
    )(*scalars, *operands)


def unset(*leaves):
    return pl.pallas_call(
        lambda *refs: None,
        out_shape=tuple(jax.ShapeDtypeStruct(shape, kind) for shape, kind in leaves),
        out_specs=(ANY_SPEC,) * len(leaves),
        name="unset",
    )()


def shards(tokens, tangent, w_up, w_down, w_router, norm_gain, route_ids):
    micro_count, tok_width, width = tokens.shape
    pipe_count = lax.axis_size("pipe")
    section = lax.axis_index("pipe")
    rank = lax.axis_index("expert")
    expert_y = rank // SIDE
    place_z = rank % SIDE
    w_in = w_up[0]
    w_out = w_down[0]
    gain = norm_gain
    router = jnp.pad(w_router[0], ((0, 0), (0, LANES - EXPERTS)))
    ff = w_in.shape[1]
    rows = SIDE * tok_width
    total = SIDE * rows

    ids = route_ids[0].reshape(micro_count, SIDE, SIDE, tok_width, 2)
    ids = ids.transpose(0, 2, 1, 3, 4).reshape(micro_count, SIDE, rows, 2)
    relative = (place_z - jnp.arange(SIDE)) % SIDE
    ids = jnp.take(ids, relative, axis=1).reshape(micro_count, total, 2)
    lane = jnp.arange(LANES, dtype=jnp.int32)
    contrast = (ids[:, :, 0:1] == lane).astype(F32) - (ids[:, :, 1:2] == lane).astype(F32)
    contrast, router = lax.optimization_barrier((contrast, router))

    start = jnp.stack([tokens, tangent], axis=1)
    groups = [[SIDE * y + z for y in range(SIDE)] for z in range(SIDE)]
    start = lax.all_gather(start, "expert", axis=2, tiled=True, axis_index_groups=groups)

    def reduce_all(parts):
        got = [z_send(parts[4 - d], d) for d in (2, 1, 3)]
        mine = parts[0].astype(F32) + got[0].astype(F32) + got[1].astype(F32) + got[2].astype(F32)
        mine = mine.astype(BF)
        return [mine] + [y_send(mine, d) for d in (2, 1, 3)]

    def make_idx(micro_idx, slot):
        return jnp.stack([micro_idx, expert_y, slot]).astype(jnp.int32)

    def plan(step):
        micro_idx = step // 2
        active = (step >= 0) & (step % 2 == 0) & (micro_idx < micro_count)
        return active, jnp.clip(micro_idx, 0, micro_count - 1)

    def forward_plan(tick):
        return plan(tick - section)

    def backward_plan(tick):
        return plan(tick - (2 * pipe_count - 1 - section))

    def fresh(tick):
        micro_idx = jnp.clip((tick + 1) // 2, 0, micro_count - 1)
        return lax.dynamic_index_in_dim(start, micro_idx, 0, keepdims=False)

    last = section == pipe_count - 1

    def forward_run(micro_idx, blocks, stores):
        parts, stores = run_forward(
            make_idx(micro_idx, 0), blocks, contrast, gain, router, w_in, w_out, stores
        )
        out = run_finish(forward_finish, "forward_finish", (), blocks[0], *reduce_all(parts))
        return out, stores

    def backward_run(micro_idx, slot, blocks, stores):
        idx = make_idx(micro_idx, slot)
        *parts, inputs = run_backward(idx, blocks, contrast, router, w_in, w_out, stores)
        return run_finish(
            backward_finish, "backward_finish", (idx,), blocks[0], inputs, gain, *reduce_all(parts)
        )

    def either_half(tick, parity, blocks, stores):
        forward_active, forward_idx = forward_plan(tick)
        backward_active, backward_idx = backward_plan(tick)

        def rest(blocks, stores):
            return jnp.zeros_like(blocks[0]) if parity else blocks[0], stores

        def forward(blocks, stores):
            return forward_run(forward_idx, blocks, stores)

        def backward(blocks, stores):
            slot = last.astype(jnp.int32)
            return backward_run(backward_idx, slot, blocks, stores), stores

        branch = jnp.where(forward_active, 1, jnp.where(backward_active, 2, 0))
        return lax.switch(branch, (rest, forward, backward), blocks, stores)

    def store_probe(tick, result, probe_store):
        active, micro_idx = backward_plan(tick)
        write_idx = jnp.where(active, micro_idx, micro_count)
        return lax.dynamic_update_index_in_dim(probe_store, result, write_idx, 0)

    *stores, probe_store = unset(
        ((36 * micro_count, rows, width), BF),
        ((7 * micro_count, total, ff), F32),
        ((14 * micro_count, total, ff), BF),
        ((36 * micro_count, 3, total, LANES), F32),
        ((10 * micro_count, rows, width), BF),
    )
    stores = tuple(stores)
    def forward_ticks(pair_idx, state):
        send, stores = state
        plans = []
        for parity in range(2):
            tick = 2 * pair_idx + parity
            active, micro_idx = forward_plan(tick)
            plans.append((make_idx(micro_idx, active), active, tick))
        send, plans = lax.optimization_barrier((send, plans))
        for parity in range(2):
            idx, active, tick = plans[parity]
            blocks = pipe_gather(send, FORWARD_HOPS[parity])
            weights = load_weights(idx, w_in, w_out)
            parts, stores = run_forward(
                idx, blocks, contrast, gain, router, *weights, stores, loaded=True
            )

            parts, active, tick = lax.optimization_barrier((parts, active, tick))

            def run(block, parts, tick):
                return run_finish(forward_finish, "forward_finish", (), block, *reduce_all(parts))

            def rest(block, parts, tick):
                return jnp.where(last, fresh(tick), block)

            send = lax.cond(active, run, rest, blocks[0], parts, tick)
        return send, stores

    def both_ticks(pair_idx, state):
        send, stores, probe_store = state
        for parity in range(2):
            tick = 2 * pair_idx + parity
            blocks = pipe_gather(send, SWAP_HOPS[parity])
            probe_store = store_probe(tick - 1, send[0], probe_store)
            send, stores = either_half(tick, parity, blocks, stores)
        return send, stores, probe_store

    def backward_ticks(pair_idx, state):
        back, probe_store = state
        plans = []
        for parity in range(2):
            tick = 2 * pair_idx + parity
            active, micro_idx = backward_plan(tick)
            prior, prior_idx = backward_plan(tick - 1)
            write_idx = jnp.where(prior, prior_idx, micro_count)
            plans.append((make_idx(micro_idx, active), active, write_idx))
        back, plans = lax.optimization_barrier((back, plans))
        for parity in range(2):
            idx, active, write_idx = plans[parity]
            back, idx = lax.optimization_barrier((back, idx))
            result = back[0]
            blocks = pipe_gather(back, BACKWARD_HOPS[parity])
            weights = turn_weights(idx, w_in, w_out)
            *parts, inputs = run_turned(idx, blocks, contrast, router, *weights, stores)
            parts, inputs, active, write_idx = lax.optimization_barrier(
                (parts, inputs, active, write_idx)
            )

            def run(block, parts, inputs):
                return run_finish(
                    backward_finish, "backward_finish", (jnp.zeros((3,), jnp.int32),),
                    block, inputs, gain, *reduce_all([part[0] for part in parts])
                )

            back = lax.cond(active, run, lambda block, parts, inputs: block, blocks[0], parts, inputs)
            probe_store = lax.dynamic_update_index_in_dim(probe_store, result, write_idx, 0)
        return back, probe_store

    lead = pipe_count // 2
    turn = lead + micro_count - 1
    send, stores = lax.fori_loop(0, lead, forward_ticks, (start[0], stores))
    send, stores, probe_store = lax.fori_loop(lead, turn, both_ticks, (send, stores, probe_store))
    back = jnp.where(last, send[1], send[0])[None]
    back, probe_store = lax.fori_loop(
        turn, pipe_count + micro_count - 1, backward_ticks, (back, probe_store)
    )
    back = back[0]
    probe_store = store_probe(2 * pipe_count + 2 * micro_count - 3, back, probe_store)
    probes = probe_store[:micro_count].reshape(micro_count, SIDE, tok_width, width)
    probes = lax.dynamic_index_in_dim(probes, expert_y, 1, keepdims=False)
    return probes[None]


def solution(mesh):
    in_specs = (
        P(None, "expert", None),
        P(None, "expert", None),
        P("pipe", None, "expert"),
        P("pipe", "expert", None),
        P("pipe", None, None),
        P("pipe", None),
        P("pipe", None, None, None),
    )
    out_specs = P("pipe", None, "expert", None)
    return jax.shard_map(shards, mesh=mesh, in_specs=in_specs, out_specs=out_specs, check_vma=False)
```
